256 devices in a mesh: wide: 128 (over x, y, z_lo, core), section: 2 (over z_hi).
Axes of the slice: x: 4, y: 4, z: 8 (z_hi: 2, z_lo: 4; z = z_hi * 4 + z_lo), core: 2. Of those that a mesh axis runs over, the one named last changes fastest.
Arguments:
- potential: float32 [4, 512, 16384], P('section', 'wide'), may hold values from -6 to 6
- speed_x: float32 [512, 16384], P('wide'), may hold values from 0.5 to 2
- speed_y: float32 [512, 16384], P('wide'), may hold values from 0.5 to 2
- density: float32 [512, 16384], P('wide'), may hold values from 0 to 2
- sign_x: int32 [4, 512, 16384], P('section', 'wide'), may hold values 0 or 1
- sign_y: int32 [4, 512, 16384], P('section', 'wide'), may hold values 0 or 1
- stem_weight: bfloat16 [45, 128], replicated, may hold values from -0.875 to 0.875
- conv_weight: bfloat16 [1, 3, 128], replicated, may hold values from -3.5 to 3.5
- norm_gain: float32 [1, 128], replicated, may hold values from 0.1 to 1.9
- up_weight: bfloat16 [1, 128, 256], replicated, may hold values from -0.5 to 0.5
- down_weight: bfloat16 [1, 256, 128], replicated, may hold values from -0.375 to 0.375
- out_weight: bfloat16 [128, 4], replicated, may hold values from -0.5 to 0.5
Outputs:
- corrected: float32 [4, 512, 16384], P(None, ('wide', 'section'))
The draws below stay inside these ranges and needn't reach their ends.
All inputs are finite; a program needn't handle non-finite values. No bound on the sum of `sign_x` or of `sign_y` on one device may be relied on, other than what follows from the above.
Results may differ from the reference program's by a relative error of at most 0.003.
Values may be sent and summed in bfloat16 or wider, within the bound.
No kernel may reach another device: no remote copies, remote signals or barrier semaphores. Data moves between devices by JAX's collectives and lax.ppermute only.
A program may use at most 64 MiB of HBM per device.

```python
import jax
import jax.numpy as jnp
from jax import lax

G = 4
FEAT = 5
C = 128
HID = 256
LAYERS = 1
NX = 16384
NY = 512


def plant(values, rng, low, largest):
    extent = values.shape
    place = [jax.random.randint(jax.random.fold_in(rng, axis), (), 0, extent[axis]) for axis in range(len(extent))]
    values = values.at[tuple(place)].set(low)
    longest = extent.index(max(extent))
    place[longest] = (place[longest] + 1) % extent[longest]
    return values.at[tuple(place)].set(largest)


def block_scale(own_key, shape, split, least, largest):
    level = 1.0
    for position, shards_of in split:
        steps = jax.random.uniform(jax.random.fold_in(jax.random.fold_in(own_key, 6), position), (shards_of,), jnp.float32, least / len(split), largest / len(split))
        level = level * jnp.repeat(jnp.exp(steps), shape[position] // shards_of).reshape((-1,) + (1,) * (len(shape) - 1 - position))
    return level


def bell_draw(key, shape, scale, most, cuts=(), kind=jnp.bfloat16):
    level = block_scale(key, shape, cuts, -0.22, 0.18) if cuts else 1.0
    drawn = jax.random.normal(key, shape, jnp.float32) * scale * level
    return jnp.minimum(jnp.maximum(drawn, -most), most).astype(kind)


def setup_inputs(seed: int = 0) -> dict:
    streams_of = jax.random.split(jax.random.key(seed), 13)
    potential = bell_draw(streams_of[0], (G, NY, NX), 1.0, 6.0, ((0, 2), (1, 128)), jnp.float32)
    speed_x = jnp.clip(0.5 + 1.5 * jax.random.uniform(streams_of[1], (NY, NX), jnp.float32) ** block_scale(streams_of[1], (NY, NX), ((0, 128),), -0.2, 0.2), 0.5, 2.0)
    speed_y = jnp.clip(0.5 + 1.5 * jax.random.uniform(streams_of[2], (NY, NX), jnp.float32) ** block_scale(streams_of[2], (NY, NX), ((0, 128),), -0.2, 0.2), 0.5, 2.0)
    density = jnp.clip(2.0 * jax.random.uniform(streams_of[3], (NY, NX), jnp.float32) ** block_scale(streams_of[3], (NY, NX), ((0, 128),), -0.2, 0.2), 0.0, 2.0)
    sign_x = plant((jax.random.randint(streams_of[4], (G, NY, NX), 0, 2) < 1).astype(jnp.int32), jax.random.fold_in(streams_of[4], 1), 0, 1)
    sign_y = plant((jax.random.randint(streams_of[5], (G, NY, NX), 0, 2) < 1).astype(jnp.int32), jax.random.fold_in(streams_of[5], 1), 0, 1)
    stem_weight = bell_draw(streams_of[6], (9 * FEAT, C), (9 * FEAT) ** -0.5, 0.875)
    conv_weight = bell_draw(streams_of[7], (LAYERS, 3, C), 3 ** -0.5, 3.5)
    norm_gain = jnp.clip(1.0 + 0.18 * jax.random.normal(streams_of[8], (LAYERS, C), jnp.float32), 0.1, 1.9)
    up_weight = bell_draw(streams_of[9], (LAYERS, C, HID), C ** -0.5, 0.5)
    down_weight = bell_draw(streams_of[10], (LAYERS, HID, C), HID ** -0.5, 0.375)
    out_weight = bell_draw(streams_of[11], (C, G), C ** -0.5, 0.5)
    return dict(potential=potential, speed_x=speed_x, speed_y=speed_y, density=density, sign_x=sign_x, sign_y=sign_y, stem_weight=stem_weight, conv_weight=conv_weight, norm_gain=norm_gain, up_weight=up_weight, down_weight=down_weight, out_weight=out_weight)


CENTRAL = (1.0 / 280.0, -4.0 / 105.0, 0.2, -0.8, 0.0, 0.8, -0.2, 4.0 / 105.0, -1.0 / 280.0)
BINOMIAL = (1.0, -8.0, 28.0, -56.0, 70.0, -56.0, 28.0, -8.0, 1.0)
DAMPING = 1.0 / 630.0
TIME_STEP = 0.6
EPSILON = 1e-06

def banded_valid(extended, along, length):
    window = lax.slice_in_dim(extended, 0, length, axis=along)
    central = CENTRAL[0] * window
    damping = BINOMIAL[0] * window
    for offset in range(1, 9):
        window = lax.slice_in_dim(extended, offset, offset + length, axis=along)
        central = central + CENTRAL[offset] * window
        damping = damping + BINOMIAL[offset] * window
    return (central, damping)

def banded(source, along):
    widths = [(0, 0)] * source.ndim
    widths[along] = (4, 4)
    return banded_valid(jnp.pad(source, widths), along, source.shape[along])

def upwind(source, central, damping, signs, speeds):
    gradient = central + (2.0 * signs - 1.0) * DAMPING * damping
    return source - TIME_STEP * speeds * gradient

def product(left, right):
    return jnp.dot(left.astype(jnp.float32), right.astype(jnp.float32), preferred_element_type=jnp.float32)

def correct_row(window, stem_weight, conv_weight, norm_gain, up_weight, down_weight, out_weight):
    count = window.shape[2] - 2
    pieces = [window[:, row_shift, col_shift:col_shift + count] for row_shift in range(3) for col_shift in range(3)]
    patches = jnp.transpose(jnp.concatenate(pieces, axis=0))
    hidden = product(patches, stem_weight)
    for layer_index in range(conv_weight.shape[0]):
        kernel = conv_weight[layer_index].astype(jnp.float32)
        padded = jnp.pad(hidden, ((1, 1), (0, 0)))
        mixed_rows = kernel[0] * padded[:-2] + kernel[1] * padded[1:-1] + kernel[2] * padded[2:]
        inverse_rms = lax.rsqrt(lax.optimization_barrier(jnp.mean(mixed_rows * mixed_rows, axis=-1, keepdims=True)) + EPSILON)
        normed = (mixed_rows * inverse_rms * norm_gain[layer_index]).astype(jnp.bfloat16)
        lifted = jax.nn.gelu(product(normed, up_weight[layer_index])).astype(jnp.bfloat16)
        hidden = hidden + product(lifted, down_weight[layer_index])
    return jnp.transpose(product(hidden.astype(jnp.bfloat16), out_weight))

def reference(potential, speed_x, speed_y, density, sign_x, sign_y, stem_weight, conv_weight, norm_gain, up_weight, down_weight, out_weight):
    central, damping = banded(potential, 2)
    swept_x = upwind(potential, central, damping, sign_x.astype(jnp.float32), speed_x[None])
    central, damping = banded(swept_x, 1)
    swept_y = upwind(swept_x, central, damping, sign_y.astype(jnp.float32), speed_y[None])
    physics = swept_y + TIME_STEP * density[None]
    features = jnp.concatenate([physics, density[None]], axis=0).astype(jnp.bfloat16)
    padded = jnp.pad(features, ((0, 0), (1, 1), (1, 1)))

    def one_row(row_index):
        window = lax.dynamic_slice_in_dim(padded, row_index, 3, 1)
        return correct_row(window, stem_weight, conv_weight, norm_gain, up_weight, down_weight, out_weight)
    corrections = lax.map(one_row, jnp.arange(physics.shape[1], dtype=jnp.int32))
    return physics + jnp.transpose(corrections, (1, 0, 2))
```

```python
import functools

import jax
import jax.numpy as jnp
from jax import lax
from jax.experimental import pallas as pl
from jax.experimental.pallas import tpu as pltpu
from jax.sharding import PartitionSpec as P

CENTRAL = (0.8, -0.2, 4.0 / 105.0, -1.0 / 280.0)
BINOMIAL = (70.0, -56.0, 28.0, -8.0, 1.0)
DAMPING = 1.0 / 630.0
TIME_STEP = 0.6
EPSILON = 1e-06
GELU_0 = 0.7978845608028654
GELU_1 = GELU_0 * 0.044715
BF16 = jnp.bfloat16
F32 = jnp.float32
BOTH = ("wide", "section")
HALO = 128


def steps(length, size, body):
    def step(index, carry):
        body(pl.multiple_of(index * size, size))
        return carry

    lax.fori_loop(0, length // size, step, 0)


def upwind_change(center, pairs, signs, speeds):
    central = jnp.zeros_like(center)
    damping = BINOMIAL[0] * center
    for k, (before, after) in enumerate(pairs, 1):
        central = central + CENTRAL[k - 1] * (after - before)
        damping = damping + BINOMIAL[k] * (after + before)
    gradient = central + (2.0 * signs - 1.0) * (DAMPING * damping)
    return (TIME_STEP * speeds) * gradient


def stacked(first, second):
    return jnp.concatenate([first, second], axis=0)


def by_row(value, row):
    roll = functools.partial(pltpu.roll, axis=0)
    placed = value
    for r in range(1, 4):
        placed = jnp.where(row == 2 * r, roll(value, r), placed)
        placed = jnp.where(row == 2 * r - 1, roll(value, 4 + r), placed)
    return placed


def sweep_x(size, pot_ref, speed_ref, sign_ref, wide_ref, narrow_ref, padded):
    length = pot_ref.shape[2]
    padded[:, :HALO] = jnp.zeros((8, HALO), F32)
    padded[:, HALO + length :] = jnp.zeros((8, HALO), F32)
    padded[0:4, HALO : HALO + length] = pot_ref[0]
    padded[4:8, HALO : HALO + length] = pot_ref[1]

    def body(start):
        here = pl.ds(start, size)
        value = padded[:, pl.ds(start, size + 2 * HALO)]
        sign = stacked(sign_ref[0, :, here], sign_ref[1, :, here]).astype(F32)
        speed = stacked(speed_ref[:, here], speed_ref[:, here])

        def at(k):
            return value[:, HALO + k : HALO + k + size]

        swept = at(0) - upwind_change(at(0), [(at(-k), at(k)) for k in range(1, 5)], sign, speed)
        wide_ref[:, here] = swept
        narrow_ref[:, here] = swept.astype(BF16)

    steps(length, size, body)


def sweep_y(
    size,
    own_ref,
    chip_ref,
    far_ref,
    speed_ref,
    sign_ref,
    density_ref,
    own_rows_ref,
    inner_ref,
    outer_ref,
    swap_ref,
    edge_ref,
    cross_ref,
):
    odd = lax.rem(lax.axis_index("wide"), 2) == 1
    low = lax.axis_index("section") == 0

    def body(start):
        here = pl.ds(start, size)
        own, chip, far = own_ref[:, here], chip_ref[:, here], far_ref[:, here].astype(F32)
        below = jnp.where(odd, chip, far)
        above = jnp.where(odd, far, chip)
        sign = stacked(sign_ref[0, :, here], sign_ref[1, :, here]).astype(F32)
        speed = stacked(speed_ref[:, here], speed_ref[:, here])
        crowd = density_ref[:, here]
        density = stacked(crowd, crowd)
        row = lax.broadcasted_iota(jnp.int32, (8, size), 0)
        in_group = row % 4
        roll = functools.partial(pltpu.roll, axis=0)
        pairs = []
        for k in range(1, 5):
            if k == 4:
                pairs.append((below, above))
            else:
                before = jnp.where(in_group < 4 - k, own, below)
                before = jnp.where(in_group >= k, roll(before, k), roll(before, 4 + k))
                after = jnp.where(in_group >= k, own, above)
                after = jnp.where(in_group < 4 - k, roll(after, 8 - k), roll(after, 4 - k))
                pairs.append((before, after))
        physics = own - upwind_change(own, pairs, sign, speed) + TIME_STEP * density
        physics = by_row(physics, row)
        crowd = jnp.where(row >= 4, density, 0.0)
        up_2, up_4, up_6 = roll(physics, 2), roll(physics, 4), roll(physics, 6)
        own_rows_ref[:, here] = jnp.where(low, physics, up_4)[0:4]
        window = jnp.where(row < 6, jnp.where(low, physics, up_6), 0.0)
        window_crowd = jnp.where(low, crowd, roll(crowd, 7))
        inner_ref[:, here] = jnp.concatenate([window, window_crowd], axis=0).astype(BF16)
        flipped = jnp.where(low, up_2, jnp.where(row < 4, up_4, physics))
        flipped_crowd = jnp.where(low, crowd, jnp.where(row == 4, roll(crowd, 5), roll(crowd, 7)))
        outer_ref[:, here] = jnp.concatenate([flipped, flipped_crowd], axis=0).astype(BF16)
        given = jnp.where(low, up_6, physics).astype(BF16)
        for j in range(3):
            swap_ref[j, :, here] = given[2 * j : 2 * j + 2]
        edge = jnp.where(low, up_2, physics)
        edge_crowd = jnp.where(low, roll(crowd, 3), roll(crowd, 6))
        edge = jnp.where(row < 2, edge, jnp.where(row == 2, edge_crowd, 0.0))
        edge_ref[:, here] = edge[0:4].astype(BF16)
        cross_ref[:, here] = jnp.where(low, physics, up_2)[0:2].astype(BF16)

    steps(own_ref.shape[1], size, body)


def correct_chunk(size, start, last, features, mix_ref, fix_ref, gain_ref, up_ref, down_ref):
    value = features[:, pl.ds(start, size + 2 * HALO)]
    patches = jnp.concatenate(
        [value[:, HALO + k : HALO + k + size] for k in range(-2, 3)], axis=0
    )
    mixed = jnp.dot(
        mix_ref[...], jnp.concatenate([patches, patches], axis=0), preferred_element_type=F32
    )
    lane = lax.broadcasted_iota(jnp.int32, (16, HALO), 1)

    def at_rim(side, keep, columns):
        column = jnp.where(keep, columns.astype(F32), 0.0).astype(BF16)
        return jnp.dot(
            fix_ref[side], jnp.concatenate([column, column], axis=0), preferred_element_type=F32
        )

    first = jnp.logical_and(lane == 0, start == 0)
    final = jnp.logical_and(lane == HALO - 1, start == last)
    head = mixed[:128, :HALO] - at_rim(0, first, value[:, HALO : 2 * HALO])
    tail = mixed[:128, size - HALO :] - at_rim(1, final, value[:, size : size + HALO])
    mixed_rows = jnp.concatenate([head, mixed[:128, HALO : size - HALO], tail], axis=1)
    square = jnp.sum(mixed_rows * mixed_rows, axis=0, keepdims=True)
    inverse = lax.rsqrt(square * (1.0 / 128.0) + EPSILON)
    normed = (mixed_rows * inverse * gain_ref[...]).astype(BF16)
    lift = jnp.dot(up_ref[...], normed, preferred_element_type=F32)
    lifted = lift + lift * jnp.tanh(lift * (GELU_0 + GELU_1 * (lift * lift)))
    result = jnp.dot(down_ref[...], lifted.astype(BF16), preferred_element_type=F32)
    return mixed[128:132] + (result[0:4] + result[4:8])


def in_groups(low, own, other):
    other = other.astype(F32)
    return jnp.where(
        low, jnp.concatenate([own, other], axis=0), jnp.concatenate([other, own], axis=0)
    )


def clear_rims(features, length):
    features[:, :HALO] = jnp.zeros((16, HALO), BF16)
    features[:, HALO + length :] = jnp.zeros((16, HALO), BF16)


def correct_inner(
    size, inner_ref, swap_ref, own_rows_ref, mix_ref, fix_ref, gain_ref, up_ref, down_ref, out_ref, features
):
    length = inner_ref.shape[1]
    low = lax.axis_index("section") == 0
    mid = slice(HALO, HALO + length)
    clear_rims(features, length)
    features[:, mid] = inner_ref[...]
    for j in range(3):
        features[6 + 2 * j : 8 + 2 * j, mid] = swap_ref[j]

    def body(start):
        here = pl.ds(start, size)
        change = correct_chunk(
            size, start, length - size, features, mix_ref, fix_ref, gain_ref, up_ref, down_ref
        )
        own = jnp.where(low, own_rows_ref[2:4, here], own_rows_ref[0:2, here])
        out_ref[:, here] = change + in_groups(low, own, swap_ref[1, :, here])

    steps(length, size, body)


def correct_outer(
    size,
    outer_ref,
    swap_ref,
    edge_ref,
    cross_ref,
    own_rows_ref,
    row_ref,
    mix_ref,
    fix_ref,
    gain_ref,
    up_ref,
    down_ref,
    out_ref,
    features,
):
    length = outer_ref.shape[1]
    low = lax.axis_index("section") == 0
    mid = slice(HALO, HALO + length)
    clear_rims(features, length)
    features[:, mid] = outer_ref[...]
    features[0:2, mid] = edge_ref[0:2]
    features[14:16, mid] = edge_ref[2:4]
    features[6:8, mid] = cross_ref[...]
    features[10:12, mid] = swap_ref[1]

    @pl.when(low)
    def _():
        features[8:10, mid] = swap_ref[0]

    @pl.when(jnp.logical_not(low))
    def _():
        features[8:10, mid] = swap_ref[2]

    def body(start):
        here = pl.ds(start, size)
        change = correct_chunk(
            size, start, length - size, features, mix_ref, fix_ref, gain_ref, up_ref, down_ref
        )
        own = jnp.where(low, own_rows_ref[0:2, here], own_rows_ref[2:4, here])
        other = jnp.where(
            low, swap_ref[0, :, here].astype(F32), swap_ref[2, :, here].astype(F32)
        )
        outer_row = change + in_groups(low, own, other)
        inner_row = row_ref[:, here]
        out_ref[:, 0, here] = jnp.where(low, outer_row, inner_row)
        out_ref[:, 1, here] = jnp.where(low, inner_row, outer_row)

    steps(length, size, body)


def halves(value):
    high = lax.reduce_precision(value, 8, 7)
    return high.astype(BF16), (value - high).astype(BF16)


def weights(low, stem_weight, conv_weight, norm_gain, up_weight, down_weight, out_weight):
    exact = functools.partial(jnp.dot, precision=lax.Precision.HIGHEST)
    channels = stem_weight.shape[1]
    stem = stem_weight.astype(F32).reshape(3, 3, 5, channels)
    conv = conv_weight[0].astype(F32)
    out = out_weight.astype(F32)
    groups = out.shape[1]
    mix = sum(
        jnp.pad(conv[s] * stem, ((0, 0), (s, 2 - s), (0, 0), (0, 0))) for s in range(3)
    )
    direct = jnp.pad(exact(stem.reshape(-1, channels), out), ((0, 0), (0, 8 - groups)))
    direct = jnp.pad(direct.reshape(3, 3, 5, 8), ((0, 0), (1, 1), (0, 0), (0, 0)))
    rims = [conv[0] * stem[:, 2], conv[2] * stem[:, 0]]
    whole = jnp.concatenate([mix, direct], axis=3)
    whole = jnp.concatenate(
        [whole] + [jnp.pad(rim, ((0, 0), (0, 0), (0, 8)))[:, None] for rim in rims], axis=1
    )

    def arranged(value, flip):
        if flip:
            value = jnp.where(low, value, value[::-1])
        fields, crowd = value[:, :, :4], value[:, :, 4]
        fields = fields.reshape(3, 7, 2, 2, -1)
        fields = jnp.where(low, fields, fields[:, :, ::-1])
        fields = jnp.transpose(fields, (1, 2, 0, 3, 4)).reshape(7, 12, -1)
        crowd = jnp.transpose(crowd, (1, 0, 2))
        if flip:
            crowd = jnp.concatenate([crowd[:, 1:], crowd[:, :1]], axis=1)
        rows = jnp.pad(jnp.concatenate([fields, crowd], axis=1), ((0, 0), (0, 1), (0, 0)))
        high, lower = halves(rows)
        mixing = jnp.concatenate([high[:5].reshape(80, -1), lower[:5].reshape(80, -1)], axis=0)
        rim = jnp.concatenate([high[5:], lower[5:]], axis=1)[:, :, :channels]
        return jnp.transpose(mixing), jnp.transpose(rim, (0, 2, 1))

    down = 0.5 * exact(down_weight[0].astype(F32), out)
    down = jnp.transpose(jnp.concatenate(halves(down), axis=1))
    shared = (jnp.transpose(norm_gain), jnp.transpose(up_weight[0]), down)
    return arranged(whole, False) + shared, arranged(whole, True) + shared


def shards(
    potential,
    speed_x,
    speed_y,
    density,
    sign_x,
    sign_y,
    stem_weight,
    conv_weight,
    norm_gain,
    up_weight,
    down_weight,
    out_weight,
):
    length = potential.shape[2]
    size = min(length, 1024)
    chunk = min(length, 512)
    low = lax.axis_index("section") == 0
    blocks = lax.axis_size("wide")
    shape = jax.ShapeDtypeStruct

    def swaps(first):
        pairs = [(2 * w + s, 2 * w + 2 + s) for w in range(first, blocks - 1, 2) for s in (0, 1)]
        return pairs + [(b, a) for a, b in pairs]

    swept, narrow = pl.pallas_call(
        functools.partial(sweep_x, size),
        out_shape=(shape((8, length), F32), shape((8, length), BF16)),
        scratch_shapes=[
            pltpu.VMEM((8, length + 2 * HALO), F32),
        ],
        name="sweep_x",
    )(potential, speed_x, sign_x)
    far = lax.ppermute(narrow, BOTH, swaps(1))
    chip = lax.ppermute(swept, BOTH, swaps(0))
    own_rows, inner, outer, given, edge, cross = pl.pallas_call(
        functools.partial(sweep_y, size),
        out_shape=(
            shape((4, length), F32),
            shape((16, length), BF16),
            shape((16, length), BF16),
            shape((3, 2, length), BF16),
            shape((4, length), BF16),
            shape((2, length), BF16),
        ),
        name="sweep_y",
    )(swept, chip, far, speed_y, sign_y, density)
    swap = lax.ppermute(given, "section", [(0, 1), (1, 0)])
    edge = lax.ppermute(
        edge,
        BOTH,
        [(2 * w + 1, 2 * w - 1) for w in range(1, blocks)]
        + [(2 * w, 2 * w + 2) for w in range(blocks - 1)],
    )
    cross = lax.ppermute(
        cross,
        BOTH,
        [(2 * w, 2 * w - 1) for w in range(1, blocks)]
        + [(2 * w + 1, 2 * w + 2) for w in range(blocks - 1)],
    )
    inner_weights, outer_weights = weights(
        low, stem_weight, conv_weight, norm_gain, up_weight, down_weight, out_weight
    )
    scratch = [pltpu.VMEM((16, length + 2 * HALO), BF16)]
    row = pl.pallas_call(
        functools.partial(correct_inner, chunk),
        out_shape=shape((4, length), F32),
        scratch_shapes=scratch,
        name="correct_inner",
    )(inner, swap, own_rows, *inner_weights)
    return pl.pallas_call(
        functools.partial(correct_outer, chunk),
        out_shape=shape((4, 2, length), F32),
        scratch_shapes=scratch,
        name="correct_outer",
    )(outer, swap, edge, cross, own_rows, row, *outer_weights)


def solution(mesh):
    placed = (
        P("section", "wide", None),
        P("wide", None),
        P("wide", None),
        P("wide", None),
        P("section", "wide", None),
        P("section", "wide", None),
        P(),
        P(),
        P(),
        P(),
        P(),
        P(),
    )
    return jax.shard_map(
        shards,
        mesh=mesh,
        in_specs=placed,
        out_specs=P(None, ("wide", "section"), None),
        check_vma=False,
    )
```

```python
import functools

import jax
import jax.numpy as jnp
import numpy as np
from jax import lax
from jax.experimental import pallas as pl
from jax.experimental.pallas import tpu as pltpu
from jax.sharding import PartitionSpec as P

CENTRAL = (0.8, -0.2, 4.0 / 105.0, -1.0 / 280.0)
BINOMIAL = (70.0, -56.0, 28.0, -8.0, 1.0)
DAMPING = 1.0 / 630.0
TIME_STEP = 0.6
EPSILON = 1e-06
GELU_0 = 0.7978845608028654
GELU_1 = GELU_0 * 0.044715
BF16 = jnp.bfloat16
F32 = jnp.float32
BOTH = ("wide", "section")
HALO = 128
LAG = 2


def steps(length, size, body):
    def step(index, carry):
        body(pl.multiple_of(index * size, size))
        return carry

    lax.fori_loop(0, length // size, step, 0)


def upwind_change(center, pairs, signs, speeds):
    central = jnp.zeros_like(center)
    damping = BINOMIAL[0] * center
    for k, (before, after) in enumerate(pairs, 1):
        central = central + CENTRAL[k - 1] * (after - before)
        damping = damping + BINOMIAL[k] * (after + before)
    gradient = central + (2.0 * signs - 1.0) * (DAMPING * damping)
    return (TIME_STEP * speeds) * gradient


def stacked(first, second):
    return jnp.concatenate([first, second], axis=0)


def by_row(value, row):
    roll = functools.partial(pltpu.roll, axis=0)
    placed = value
    for r in range(1, 4):
        placed = jnp.where(row == 2 * r, roll(value, r), placed)
        placed = jnp.where(row == 2 * r - 1, roll(value, 4 + r), placed)
    return placed


def sweep_x(size, pot_ref, speed_ref, sign_ref, wide_ref, narrow_ref, padded):
    length = pot_ref.shape[2]
    padded[:, :HALO] = jnp.zeros((8, HALO), F32)
    padded[:, HALO + length :] = jnp.zeros((8, HALO), F32)
    padded[0:4, HALO : HALO + length] = pot_ref[0]
    padded[4:8, HALO : HALO + length] = pot_ref[1]

    def body(start):
        here = pl.ds(start, size)
        value = padded[:, pl.ds(start, size + 2 * HALO)]
        sign = stacked(sign_ref[0, :, here], sign_ref[1, :, here]).astype(F32)
        speed = stacked(speed_ref[:, here], speed_ref[:, here])

        def at(k):
            return value[:, HALO + k : HALO + k + size]

        swept = at(0) - upwind_change(at(0), [(at(-k), at(k)) for k in range(1, 5)], sign, speed)
        wide_ref[:, here] = swept
        narrow_ref[:, here] = swept.astype(BF16)

    steps(length, size, body)


def sweep_y(
    size,
    own_ref,
    chip_ref,
    far_ref,
    speed_ref,
    sign_ref,
    density_ref,
    own_rows_ref,
    inner_ref,
    outer_ref,
    swap_ref,
    edge_ref,
    cross_ref,
):
    odd = lax.rem(lax.axis_index("wide"), 2) == 1
    low = lax.axis_index("section") == 0

    def body(start):
        here = pl.ds(start, size)
        own, chip, far = own_ref[:, here], chip_ref[:, here], far_ref[:, here].astype(F32)
        below = jnp.where(odd, chip, far)
        above = jnp.where(odd, far, chip)
        sign = stacked(sign_ref[0, :, here], sign_ref[1, :, here]).astype(F32)
        speed = stacked(speed_ref[:, here], speed_ref[:, here])
        crowd = density_ref[:, here]
        density = stacked(crowd, crowd)
        row = lax.broadcasted_iota(jnp.int32, (8, size), 0)
        in_group = row % 4
        roll = functools.partial(pltpu.roll, axis=0)
        pairs = []
        for k in range(1, 5):
            if k == 4:
                pairs.append((below, above))
            else:
                before = jnp.where(in_group < 4 - k, own, below)
                before = jnp.where(in_group >= k, roll(before, k), roll(before, 4 + k))
                after = jnp.where(in_group >= k, own, above)
                after = jnp.where(in_group < 4 - k, roll(after, 8 - k), roll(after, 4 - k))
                pairs.append((before, after))
        physics = own - upwind_change(own, pairs, sign, speed) + TIME_STEP * density
        physics = by_row(physics, row)
        crowd = jnp.where(row >= 4, density, 0.0)
        up_2, up_4, up_6 = roll(physics, 2), roll(physics, 4), roll(physics, 6)
        own_rows_ref[:, here] = jnp.where(low, physics, up_4)[0:4]
        window = jnp.where(row < 6, jnp.where(low, physics, up_6), 0.0)
        window_crowd = jnp.where(low, crowd, roll(crowd, 7))
        inner_ref[:, here] = jnp.concatenate([window, window_crowd], axis=0).astype(BF16)
        flipped = jnp.where(low, up_2, jnp.where(row < 4, up_4, physics))
        flipped_crowd = jnp.where(low, crowd, jnp.where(row == 4, roll(crowd, 5), roll(crowd, 7)))
        outer_ref[:, here] = jnp.concatenate([flipped, flipped_crowd], axis=0).astype(BF16)
        given = jnp.where(low, up_6, physics).astype(BF16)
        for j in range(3):
            swap_ref[j, :, here] = given[2 * j : 2 * j + 2]
        edge = jnp.where(low, up_2, physics)
        edge_crowd = jnp.where(low, roll(crowd, 3), roll(crowd, 6))
        edge = jnp.where(row < 2, edge, jnp.where(row == 2, edge_crowd, 0.0))
        edge_ref[:, here] = edge[0:4].astype(BF16)
        cross_ref[:, here] = jnp.where(low, physics, up_2)[0:2].astype(BF16)

    steps(own_ref.shape[1], size, body)


def mix_features(size, start, length, features, mix_ref, fix_ref):
    value = features[:, start : start + size + 2 * HALO]
    patches = jnp.concatenate(
        [value[:, HALO + k : HALO + k + size] for k in range(-2, 3)], axis=0
    )
    mixed = jnp.dot(mix_ref[...], patches, preferred_element_type=F32)
    change = mixed[128:132] + mixed[132:136]
    mixed = mixed[:128]
    lane = lax.broadcasted_iota(jnp.int32, (16, HALO), 1)

    def at_rim(side, place, columns):
        column = jnp.where(lane == place, columns.astype(F32), 0.0).astype(BF16)
        return jnp.dot(fix_ref[side], column, preferred_element_type=F32)

    if start == 0:
        head = mixed[:, :HALO] - at_rim(0, 0, value[:, HALO : 2 * HALO])
        mixed = jnp.concatenate([head, mixed[:, HALO:]], axis=1)
    if start + size == length:
        tail = mixed[:, size - HALO :] - at_rim(1, HALO - 1, value[:, size : size + HALO])
        mixed = jnp.concatenate([mixed[:, : size - HALO], tail], axis=1)
    return mixed, change


def normalise(mixed, gain):
    square = jnp.sum(mixed * mixed, axis=0, keepdims=True)
    inverse = lax.rsqrt(square * (1.0 / 128.0) + EPSILON)
    return (mixed * inverse * gain).astype(BF16)


def lift_twice(normed, up_ref):
    lift = jnp.dot(up_ref[...], normed, preferred_element_type=F32).astype(BF16)
    inner = BF16(GELU_0) + BF16(GELU_1) * (lift * lift)
    return lift + lift * jnp.tanh(lift * inner)


def correct(size, length, features, weight_refs, finish):
    mix_ref, fix_ref, gain_ref, up_ref, down_ref = weight_refs
    gain = jnp.broadcast_to(gain_ref[...], (128, size))
    count = length // size
    mixed, normed, lifted, changes = {}, {}, {}, {}
    for t in range(count + 3 * LAG):
        if t < count:
            mixed[t], changes[t] = mix_features(
                size, t * size, length, features, mix_ref, fix_ref
            )
        u = t - 3 * LAG
        if u >= 0:
            result = jnp.dot(down_ref[...], lifted.pop(u), preferred_element_type=F32)
            finish(slice(u * size, u * size + size), changes.pop(u) + (result[0:4] + result[4:8]))
        u = t - 2 * LAG
        if 0 <= u < count:
            lifted[u] = lift_twice(normed.pop(u), up_ref)
        u = t - LAG
        if 0 <= u < count:
            normed[u] = normalise(mixed.pop(u), gain)


def in_groups(low, own, other):
    other = other.astype(F32)
    return jnp.where(
        low, jnp.concatenate([own, other], axis=0), jnp.concatenate([other, own], axis=0)
    )


def clear_rims(features, length):
    features[:, :HALO] = jnp.zeros((16, HALO), BF16)
    features[:, HALO + length :] = jnp.zeros((16, HALO), BF16)


def correct_inner(size, inner_ref, swap_ref, own_rows_ref, *refs):
    *weight_refs, out_ref, features = refs
    length = inner_ref.shape[1]
    low = lax.axis_index("section") == 0
    mid = slice(HALO, HALO + length)
    clear_rims(features, length)
    features[:, mid] = inner_ref[...]
    for j in range(3):
        features[6 + 2 * j : 8 + 2 * j, mid] = swap_ref[j]

    def finish(here, change):
        own = jnp.where(low, own_rows_ref[2:4, here], own_rows_ref[0:2, here])
        out_ref[:, here] = change + in_groups(low, own, swap_ref[1, :, here])

    correct(size, length, features, weight_refs, finish)


def correct_outer(
    size, outer_ref, swap_ref, edge_ref, cross_ref, own_rows_ref, row_ref, *refs
):
    *weight_refs, out_ref, features = refs
    length = outer_ref.shape[1]
    low = lax.axis_index("section") == 0
    mid = slice(HALO, HALO + length)
    clear_rims(features, length)
    features[:, mid] = outer_ref[...]
    features[0:2, mid] = edge_ref[0:2]
    features[14:16, mid] = edge_ref[2:4]
    features[6:8, mid] = cross_ref[...]
    features[10:12, mid] = swap_ref[1]

    @pl.when(low)
    def _():
        features[8:10, mid] = swap_ref[0]

    @pl.when(jnp.logical_not(low))
    def _():
        features[8:10, mid] = swap_ref[2]

    def finish(here, change):
        own = jnp.where(low, own_rows_ref[0:2, here], own_rows_ref[2:4, here])
        other = jnp.where(
            low, swap_ref[0, :, here].astype(F32), swap_ref[2, :, here].astype(F32)
        )
        outer_row = change + in_groups(low, own, other)
        inner_row = row_ref[:, here]
        out_ref[:, 0, here] = jnp.where(low, outer_row, inner_row)
        out_ref[:, 1, here] = jnp.where(low, inner_row, outer_row)

    correct(size, length, features, weight_refs, finish)


def selections():
    picks = np.zeros((2, 2, 6, 45, 128), np.float32)
    for section in range(2):
        for outer in range(2):
            places = []
            for row in range(3):
                for group in range(4):
                    other = int(group // 2 != section)
                    shift = 2 - row if outer and section else row
                    places.append((6 * other + 2 * row + group % 2, shift, group))
                crowd = 12 + ((row + 2) % 3 if outer else row)
                places.append((crowd, shift, 4))
            for place, shift, channel in places:
                for column in range(3):
                    source = 15 * shift + 5 * column + channel
                    for tap in range(3):
                        picks[section, outer, tap, source, 16 * (tap + column) + place] = 1.0
                    picks[section, outer, 3, source, 16 * (column + 1) + place] = 1.0
                picks[section, outer, 4, 15 * shift + 10 + channel, place] = 1.0
                picks[section, outer, 5, 15 * shift + channel, place] = 1.0
    return picks.transpose(0, 1, 3, 2, 4).reshape(2, 2, 45, 768)


def prepare(pick_ref, stem_ref, conv_ref, gain_ref, up_ref, down_ref, out_ref, *refs):
    inner_refs, outer_refs, (gain_out, up_out, down_out) = refs[0:2], refs[2:4], refs[4:7]
    section = lax.axis_index("section")

    def turned(left, right):
        return lax.dot_general(
            left, right, (((0,), (0,)), ((), ())), preferred_element_type=F32
        )

    def unit(size):
        rows = lax.broadcasted_iota(jnp.int32, (size, size), 0)
        return jnp.where(rows == lax.broadcasted_iota(jnp.int32, (size, size), 1), 1.0, 0.0)

    def split(value):
        high = value.astype(BF16)
        return high, (value - high.astype(F32)).astype(BF16)

    conv = turned(conv_ref[0], unit(3).astype(BF16))
    for outer, (mix_out, fix_out) in enumerate((inner_refs, outer_refs)):
        picked = turned(stem_ref[...], pick_ref[section, outer])
        parts = [picked[:, 128 * i : 128 * i + 128] for i in range(6)]
        mix = sum(conv[:, i : i + 1] * parts[i] for i in range(3))
        direct = turned(out_ref[...], parts[3].astype(BF16))
        rows = jnp.concatenate([mix, direct, direct - direct.astype(BF16).astype(F32)], axis=0)
        mix_out[...] = rows[:, :80].astype(BF16)
        fix_out[0] = (conv[:, 0:1] * parts[4])[:, :16].astype(BF16)
        fix_out[1] = (conv[:, 2:3] * parts[5])[:, :16].astype(BF16)
    gain_out[...] = jnp.sum(unit(128) * gain_ref[...], axis=1, keepdims=True)
    up_out[...] = turned(up_ref[0], unit(128).astype(BF16)).astype(BF16)
    down = 0.5 * lax.dot_general(
        out_ref[...], down_ref[0], (((0,), (1,)), ((), ())), preferred_element_type=F32
    )
    down_out[...] = jnp.concatenate([down, down - down.astype(BF16).astype(F32)], axis=0).astype(BF16)


def shards(
    potential,
    speed_x,
    speed_y,
    density,
    sign_x,
    sign_y,
    stem_weight,
    conv_weight,
    norm_gain,
    up_weight,
    down_weight,
    out_weight,
):
    length = potential.shape[2]
    size = min(length, 4096)
    chunk = min(length, 512)
    blocks = lax.axis_size("wide")
    shape = jax.ShapeDtypeStruct

    def swaps(first):
        pairs = [(2 * w + s, 2 * w + 2 + s) for w in range(first, blocks - 1, 2) for s in (0, 1)]
        return pairs + [(b, a) for a, b in pairs]

    swept, narrow = pl.pallas_call(
        functools.partial(sweep_x, size),
        out_shape=(shape((8, length), F32), shape((8, length), BF16)),
        scratch_shapes=[
            pltpu.VMEM((8, length + 2 * HALO), F32),
        ],
        name="sweep_x",
    )(potential, speed_x, sign_x)
    far = lax.ppermute(narrow, BOTH, swaps(1))
    chip = lax.ppermute(swept, BOTH, swaps(0))
    own_rows, inner, outer, given, edge, cross = pl.pallas_call(
        functools.partial(sweep_y, size),
        out_shape=(
            shape((4, length), F32),
            shape((16, length), BF16),
            shape((16, length), BF16),
            shape((3, 2, length), BF16),
            shape((4, length), BF16),
            shape((2, length), BF16),
        ),
        name="sweep_y",
    )(swept, chip, far, speed_y, sign_y, density)
    swap = lax.ppermute(given, "section", [(0, 1), (1, 0)])
    edge = lax.ppermute(
        edge,
        BOTH,
        [(2 * w + 1, 2 * w - 1) for w in range(1, blocks)]
        + [(2 * w, 2 * w + 2) for w in range(blocks - 1)],
    )
    cross = lax.ppermute(
        cross,
        BOTH,
        [(2 * w, 2 * w - 1) for w in range(1, blocks)]
        + [(2 * w + 1, 2 * w + 2) for w in range(blocks - 1)],
    )
    mix_shapes = (shape((136, 80), BF16), shape((2, 128, 16), BF16))
    shared_shapes = (shape((128, 1), F32), shape((256, 128), BF16), shape((8, 256), BF16))
    made = pl.pallas_call(
        prepare, out_shape=mix_shapes + mix_shapes + shared_shapes, name="prepare"
    )(
        jnp.asarray(selections(), BF16),
        stem_weight,
        conv_weight,
        norm_gain,
        up_weight,
        down_weight,
        out_weight,
    )
    inner_weights, outer_weights = made[0:2] + made[4:7], made[2:7]
    scratch = [pltpu.VMEM((16, length + 2 * HALO), BF16)]
    row = pl.pallas_call(
        functools.partial(correct_inner, chunk),
        out_shape=shape((4, length), F32),
        scratch_shapes=scratch,
        name="correct_inner",
    )(inner, swap, own_rows, *inner_weights)
    return pl.pallas_call(
        functools.partial(correct_outer, chunk),
        out_shape=shape((4, 2, length), F32),
        scratch_shapes=scratch,
        name="correct_outer",
    )(outer, swap, edge, cross, own_rows, row, *outer_weights)


def solution(mesh):
    placed = (
        P("section", "wide", None),
        P("wide", None),
        P("wide", None),
        P("wide", None),
        P("section", "wide", None),
        P("section", "wide", None),
        P(),
        P(),
        P(),
        P(),
        P(),
        P(),
    )
    return jax.shard_map(
        shards,
        mesh=mesh,
        in_specs=placed,
        out_specs=P(None, ("wide", "section"), None),
        check_vma=False,
    )
```

```python
import functools

import jax
import jax.numpy as jnp
import numpy as np
from jax import lax
from jax.experimental import pallas as pl
from jax.experimental.pallas import tpu as pltpu
from jax.sharding import PartitionSpec as P

CENTRAL = (3.0, -32.0, 168.0, -672.0, 0.0, 672.0, -168.0, 32.0, -3.0)
BINOMIAL = (1.0, -8.0, 28.0, -56.0, 70.0, -56.0, 28.0, -8.0, 1.0)
CENTRAL_UNIT = 1.0 / 840.0
DAMPING = 1.0 / 630.0
TIME_STEP = 0.6
EPSILON = 1e-06
GELU_0 = 0.7978845608028654
GELU_1 = GELU_0 * 0.044715
BF16 = jnp.bfloat16
F32 = jnp.float32
BOTH = ("wide", "section")
HALO = 128
LAG = 2


def params(**more):
    return pltpu.CompilerParams(vmem_limit_bytes=24 << 20, **more)


def stacked(first, second):
    return jnp.concatenate([first, second], axis=0)


def split(value):
    high = value.astype(BF16).astype(F32)
    return high, value - high


def change_of(central, damping, signs, speeds):
    gradient = CENTRAL_UNIT * central + ((2.0 * DAMPING) * signs - DAMPING) * damping
    return (TIME_STEP * speeds) * gradient


def band_matrix():
    bands = np.zeros((3, 128, 3, 2, 128), np.float32)
    for column in range(128):
        for k in range(-4, 5):
            block, lane = divmod(column + k, 128)
            bands[0, lane, block, 0, column] = CENTRAL[k + 4]
            bands[0, lane, block, 1, column] = BINOMIAL[k + 4]
    return bands[0].reshape(128, 768)


def sweep_x(blocks, band_ref, pot_ref, speed_ref, sign_ref, wide_ref, narrow_ref):
    count = pot_ref.shape[2] // 128
    band = stacked(band_ref[...], band_ref[...])

    def tall(value):
        return jnp.concatenate(
            [value[:, i : i + 128] for i in range(0, value.shape[1], 128)], axis=0
        )

    for first in range(0, count, blocks):
        start, stop = max(first - 1, 0), min(first + blocks + 1, count)
        around = slice(128 * start, 128 * stop)
        here = slice(128 * first, 128 * (first + blocks))
        value = tall(stacked(pot_ref[0, :, around], pot_ref[1, :, around]))
        zeros = jnp.zeros((8, 128), F32)
        if start == first:
            value = jnp.concatenate([zeros, value], axis=0)
        if stop == first + blocks:
            value = jnp.concatenate([value, zeros], axis=0)
        high, rest = split(value)
        both = jnp.concatenate([high.astype(BF16), rest.astype(BF16)], axis=1)
        parts = jnp.dot(both, band, preferred_element_type=F32)
        size = 8 * blocks
        mid, before, after = slice(8, 8 + size), slice(0, size), slice(16, 16 + size)
        total = parts[mid, :256] + parts[after, 256:512] + parts[before, 512:]
        sign = tall(stacked(sign_ref[0, :, here], sign_ref[1, :, here]).astype(F32))
        speed = tall(stacked(speed_ref[:, here], speed_ref[:, here]))
        swept = value[mid] - change_of(total[:, :128], total[:, 128:], sign, speed)
        swept = jnp.concatenate([swept[8 * i : 8 * i + 8] for i in range(blocks)], axis=1)
        wide_ref[:, here] = swept
        narrow_ref[:, here] = swept.astype(BF16)


def column_matrix():
    rows = np.zeros((2, 2, 7, 8, 64), np.float32)
    for odd in range(2):
        for section in range(2):
            part = rows[odd, section]
            for place in range(4):
                r = 3 - place if section else place
                for g in range(2):
                    at, own = 2 * place + g, 4 * g + r
                    for k in range(-4, 5):
                        block, source = divmod(r + k, 4)
                        if block == 0:
                            starts = (0, 8)
                        elif (block < 0) == bool(odd):
                            starts = (16, 24)
                        else:
                            starts = (32,)
                        for start in starts:
                            part[0, at, start + 4 * g + source] = CENTRAL[k + 4]
                            part[1, at, start + 4 * g + source] = BINOMIAL[k + 4]
                    part[2, at, [own, 8 + own]] = 1.0
                    part[3, at, 40 + own] = 1.0
                    part[4, at, [48 + r, 56 + r]] = 1.0
                    part[5, at, [52 + r, 60 + r]] = 1.0
                part[6, 4 + place, [52 + r, 60 + r]] = 1.0
    return rows.reshape(2, 2, 56, 64)


def sweep_y(
    size,
    column_ref,
    own_ref,
    chip_ref,
    far_ref,
    speed_ref,
    sign_ref,
    density_ref,
    own_rows_ref,
    inner_ref,
    outer_ref,
    swap_ref,
    edge_ref,
    cross_ref,
):
    columns = column_ref[lax.rem(lax.axis_index("wide"), 2), lax.axis_index("section")]
    row = lax.broadcasted_iota(jnp.int32, (8, size), 0)
    for start in range(0, own_ref.shape[1], size):
        here = slice(start, start + size)
        sign = stacked(sign_ref[0, :, here], sign_ref[1, :, here]).astype(F32)
        sources = (
            split(own_ref[:, here])
            + split(chip_ref[:, here])
            + (far_ref[:, here].astype(F32), sign)
            + split(stacked(speed_ref[:, here], density_ref[:, here]))
        )
        sources = jnp.concatenate(
            [stacked(sources[i], sources[i + 1]).astype(BF16) for i in range(0, 8, 2)], axis=0
        )
        parts = jnp.dot(columns, sources, preferred_element_type=F32)
        central, damping, own, sign, speed, density, crowd = (
            parts[8 * i : 8 * i + 8] for i in range(7)
        )
        physics = own - change_of(central, damping, sign, speed) + TIME_STEP * density
        turned = pltpu.roll(physics, 2, axis=0)
        own_rows_ref[:, here] = physics[0:4]
        inner_ref[:, here] = stacked(physics, crowd).astype(BF16)
        outer_ref[:, here] = stacked(turned, crowd).astype(BF16)
        narrow = physics.astype(BF16)
        for j in range(3):
            swap_ref[j, :, here] = narrow[2 * j + 2 : 2 * j + 4]
        edge = jnp.where(row < 2, turned, pltpu.roll(crowd, 3, axis=0))
        edge_ref[:, here] = edge[0:4].astype(BF16)
        cross_ref[:, here] = narrow[0:2]


def mix_features(size, start, length, features, mix_ref, fix_ref):
    value = features[:, start : start + size + 2 * HALO]
    patches = jnp.concatenate(
        [value[:, HALO + k : HALO + k + size] for k in range(-2, 3)], axis=0
    )
    mixed = jnp.dot(mix_ref[...], patches, preferred_element_type=F32)
    change = mixed[128:132] + mixed[132:136]
    mixed = mixed[:128]
    lane = lax.broadcasted_iota(jnp.int32, (16, HALO), 1)

    def at_rim(side, place, columns):
        column = jnp.where(lane == place, columns.astype(F32), 0.0).astype(BF16)
        return jnp.dot(fix_ref[side], column, preferred_element_type=F32)

    if start == 0:
        head = mixed[:, :HALO] - at_rim(0, 0, value[:, HALO : 2 * HALO])
        mixed = jnp.concatenate([head, mixed[:, HALO:]], axis=1)
    if start + size == length:
        tail = mixed[:, size - HALO :] - at_rim(1, HALO - 1, value[:, size : size + HALO])
        mixed = jnp.concatenate([mixed[:, : size - HALO], tail], axis=1)
    return mixed, change


def normalise(mixed, gain):
    square = jnp.sum(mixed * mixed, axis=0, keepdims=True)
    inverse = lax.rsqrt(square * (1.0 / 128.0) + EPSILON)
    return (mixed * inverse * gain).astype(BF16)


def lift_twice(normed, up_ref):
    lift = jnp.dot(up_ref[...], normed, preferred_element_type=F32).astype(BF16)
    inner = BF16(GELU_0) + BF16(GELU_1) * (lift * lift)
    return lift + lift * jnp.tanh(lift * inner)


def correct(size, length, features, weight_refs, finish):
    mix_ref, fix_ref, gain_ref, up_ref, down_ref = weight_refs
    gain = jnp.broadcast_to(gain_ref[...], (128, size))
    count = length // size
    mixed, normed, lifted, changes = {}, {}, {}, {}
    for t in range(count + 3 * LAG):
        if t < count:
            mixed[t], changes[t] = mix_features(
                size, t * size, length, features, mix_ref, fix_ref
            )
        u = t - 3 * LAG
        if u >= 0:
            result = jnp.dot(down_ref[...], lifted.pop(u), preferred_element_type=F32)
            finish(slice(u * size, u * size + size), changes.pop(u) + (result[0:4] + result[4:8]))
        u = t - 2 * LAG
        if 0 <= u < count:
            lifted[u] = lift_twice(normed.pop(u), up_ref)
        u = t - LAG
        if 0 <= u < count:
            normed[u] = normalise(mixed.pop(u), gain)


def in_groups(low, own, other):
    other = other.astype(F32)
    return jnp.where(
        low, jnp.concatenate([own, other], axis=0), jnp.concatenate([other, own], axis=0)
    )


def clear_rims(features, length):
    features[:, :HALO] = jnp.zeros((16, HALO), BF16)
    features[:, HALO + length :] = jnp.zeros((16, HALO), BF16)


def correct_inner(size, inner_ref, swap_ref, own_rows_ref, *refs):
    *weight_refs, out_ref, features = refs
    length = inner_ref.shape[1]
    low = lax.axis_index("section") == 0
    mid = slice(HALO, HALO + length)
    clear_rims(features, length)
    features[:, mid] = inner_ref[...]
    for j in range(3):
        features[6 + 2 * j : 8 + 2 * j, mid] = swap_ref[2 - j]

    def finish(here, change):
        own = own_rows_ref[2:4, here]
        out_ref[:, here] = change + in_groups(low, own, swap_ref[1, :, here])

    correct(size, length, features, weight_refs, finish)


def correct_outer(
    size, outer_ref, swap_ref, edge_ref, cross_ref, own_rows_ref, row_ref, *refs
):
    *weight_refs, out_ref, features = refs
    length = outer_ref.shape[1]
    low = lax.axis_index("section") == 0
    mid = slice(HALO, HALO + length)
    clear_rims(features, length)
    features[:, mid] = outer_ref[...]
    features[0:2, mid] = edge_ref[0:2]
    features[14:16, mid] = edge_ref[2:4]
    features[6:8, mid] = cross_ref[...]
    features[10:12, mid] = swap_ref[1]

    features[8:10, mid] = swap_ref[2]

    def finish(here, change):
        outer_row = change + in_groups(low, own_rows_ref[0:2, here], swap_ref[2, :, here])
        inner_row = row_ref[:, here]
        out_ref[:, 0, here] = jnp.where(low, outer_row, inner_row)
        out_ref[:, 1, here] = jnp.where(low, inner_row, outer_row)

    correct(size, length, features, weight_refs, finish)


def selections():
    picks = np.zeros((2, 2, 6, 45, 128), np.float32)
    for section in range(2):
        for outer in range(2):
            places = []
            for row in range(3):
                for group in range(4):
                    other = int(group // 2 != section)
                    shift = 2 - row if section else row
                    places.append((6 * other + 2 * row + group % 2, shift, group))
                crowd = 12 + ((row + 2) % 3 if outer else row)
                places.append((crowd, shift, 4))
            for place, shift, channel in places:
                for column in range(3):
                    source = 15 * shift + 5 * column + channel
                    for tap in range(3):
                        picks[section, outer, tap, source, 16 * (tap + column) + place] = 1.0
                    picks[section, outer, 3, source, 16 * (column + 1) + place] = 1.0
                picks[section, outer, 4, 15 * shift + 10 + channel, place] = 1.0
                picks[section, outer, 5, 15 * shift + channel, place] = 1.0
    return picks.transpose(0, 1, 3, 2, 4).reshape(2, 2, 45, 768)


def prepare(pick_ref, stem_ref, conv_ref, gain_ref, up_ref, down_ref, out_ref, *refs):
    inner_refs, outer_refs, (gain_out, up_out, down_out) = refs[0:2], refs[2:4], refs[4:7]
    section = lax.axis_index("section")

    def turned(left, right):
        return lax.dot_general(
            left, right, (((0,), (0,)), ((), ())), preferred_element_type=F32
        )

    def unit(size):
        rows = lax.broadcasted_iota(jnp.int32, (size, size), 0)
        return jnp.where(rows == lax.broadcasted_iota(jnp.int32, (size, size), 1), 1.0, 0.0)

    conv = turned(conv_ref[0], unit(3).astype(BF16))
    for outer, (mix_out, fix_out) in enumerate((inner_refs, outer_refs)):
        picked = turned(stem_ref[...], pick_ref[section, outer])
        parts = [picked[:, 128 * i : 128 * i + 128] for i in range(6)]
        mix = sum(conv[:, i : i + 1] * parts[i] for i in range(3))
        direct = turned(out_ref[...], parts[3].astype(BF16))
        rows = jnp.concatenate([mix, direct, direct - direct.astype(BF16).astype(F32)], axis=0)
        mix_out[...] = rows[:, :80].astype(BF16)
        fix_out[0] = (conv[:, 0:1] * parts[4])[:, :16].astype(BF16)
        fix_out[1] = (conv[:, 2:3] * parts[5])[:, :16].astype(BF16)
    gain_out[...] = jnp.sum(unit(128) * gain_ref[...], axis=1, keepdims=True)
    up_out[...] = turned(up_ref[0], unit(128).astype(BF16)).astype(BF16)
    down = 0.5 * lax.dot_general(
        out_ref[...], down_ref[0], (((0,), (1,)), ((), ())), preferred_element_type=F32
    )
    down_out[...] = jnp.concatenate([down, down - down.astype(BF16).astype(F32)], axis=0).astype(BF16)


def shards(
    potential,
    speed_x,
    speed_y,
    density,
    sign_x,
    sign_y,
    stem_weight,
    conv_weight,
    norm_gain,
    up_weight,
    down_weight,
    out_weight,
):
    length = potential.shape[2]
    size = min(length, 2048)
    chunk = min(length, 512)
    blocks = lax.axis_size("wide")
    shape = jax.ShapeDtypeStruct

    def swaps(first):
        pairs = [(2 * w + s, 2 * w + 2 + s) for w in range(first, blocks - 1, 2) for s in (0, 1)]
        return pairs + [(b, a) for a, b in pairs]

    swept, narrow = pl.pallas_call(
        functools.partial(sweep_x, size // 128),
        out_shape=(shape((8, length), F32), shape((8, length), BF16)),
        compiler_params=params(),
        name="sweep_x",
    )(jnp.asarray(band_matrix(), BF16), potential, speed_x, sign_x)
    far = lax.ppermute(narrow, BOTH, swaps(1))
    chip = lax.ppermute(swept, BOTH, swaps(0))
    mix_shapes = (shape((136, 80), BF16), shape((2, 128, 16), BF16))
    shared_shapes = (shape((128, 1), F32), shape((256, 128), BF16), shape((8, 256), BF16))
    made = pl.pallas_call(
        prepare,
        out_shape=mix_shapes + mix_shapes + shared_shapes,
        compiler_params=params(),
        name="prepare",
    )(
        jnp.asarray(selections(), BF16),
        stem_weight,
        conv_weight,
        norm_gain,
        up_weight,
        down_weight,
        out_weight,
    )
    chip, far, made = lax.optimization_barrier((chip, far, made))
    own_rows, inner, outer, given, edge, cross = pl.pallas_call(
        functools.partial(sweep_y, size),
        out_shape=(
            shape((4, length), F32),
            shape((16, length), BF16),
            shape((16, length), BF16),
            shape((3, 2, length), BF16),
            shape((4, length), BF16),
            shape((2, length), BF16),
        ),
        compiler_params=params(),
        name="sweep_y",
    )(jnp.asarray(column_matrix(), BF16), swept, chip, far, speed_y, sign_y, density)
    swap = lax.ppermute(given, "section", [(0, 1), (1, 0)])
    edge = lax.ppermute(
        edge,
        BOTH,
        [(2 * w + 1, 2 * w - 1) for w in range(1, blocks)]
        + [(2 * w, 2 * w + 2) for w in range(blocks - 1)],
    )
    cross = lax.ppermute(
        cross,
        BOTH,
        [(2 * w, 2 * w - 1) for w in range(1, blocks)]
        + [(2 * w + 1, 2 * w + 2) for w in range(blocks - 1)],
    )
    inner_weights, outer_weights = made[0:2] + made[4:7], made[2:7]
    scratch = [pltpu.VMEM((16, length + 2 * HALO), BF16)]
    row = pl.pallas_call(
        functools.partial(correct_inner, chunk),
        out_shape=shape((4, length), F32),
        scratch_shapes=scratch,
        compiler_params=params(),
        name="correct_inner",
    )(inner, swap, own_rows, *inner_weights)
    return pl.pallas_call(
        functools.partial(correct_outer, chunk),
        out_shape=shape((4, 2, length), F32),
        scratch_shapes=scratch,
        compiler_params=params(),
        name="correct_outer",
    )(outer, swap, edge, cross, own_rows, row, *outer_weights)


def solution(mesh):
    placed = (
        P("section", "wide", None),
        P("wide", None),
        P("wide", None),
        P("wide", None),
        P("section", "wide", None),
        P("section", "wide", None),
        P(),
        P(),
        P(),
        P(),
        P(),
        P(),
    )
    return jax.shard_map(
        shards,
        mesh=mesh,
        in_specs=placed,
        out_specs=P(None, ("wide", "section"), None),
        check_vma=False,
    )
```

```python
import functools

import jax
import jax.numpy as jnp
import numpy as np
from jax import lax
from jax.experimental import pallas as pl
from jax.experimental.pallas import tpu as pltpu
from jax.sharding import PartitionSpec as P

CENTRAL = (3.0, -32.0, 168.0, -672.0, 0.0, 672.0, -168.0, 32.0, -3.0)
BINOMIAL = (1.0, -8.0, 28.0, -56.0, 70.0, -56.0, 28.0, -8.0, 1.0)
CENTRAL_UNIT = 1.0 / 840.0
DAMPING = 1.0 / 630.0
TIME_STEP = 0.6
EPSILON = 1e-06
GELU_LINEAR = 0.7978845608028654
GELU_SCALE = (GELU_LINEAR * 0.044715) ** (1.0 / 3.0)
BF16 = jnp.bfloat16
F32 = jnp.float32
BOTH = ("wide", "section")
HALO = 128
LAG = 2


def params(mebibytes=24):
    return pltpu.CompilerParams(vmem_limit_bytes=mebibytes << 20)


def stacked(first, second):
    return jnp.concatenate([first, second], axis=0)


def split(value):
    high = value.astype(BF16).astype(F32)
    return high, value - high


def change_of(central, damping, signs, speeds):
    gradient = CENTRAL_UNIT * central + ((2.0 * DAMPING) * signs - DAMPING) * damping
    return (TIME_STEP * speeds) * gradient


def band_matrix():
    bands = np.zeros((3, 128, 3, 2, 128), np.float32)
    for column in range(128):
        for k in range(-4, 5):
            block, lane = divmod(column + k, 128)
            bands[0, lane, block, 0, column] = CENTRAL[k + 4]
            bands[0, lane, block, 1, column] = BINOMIAL[k + 4]
    return bands[0].reshape(128, 768)


def sweep_x(
    blocks,
    band_hbm,
    pot_hbm,
    speed_hbm,
    sign_hbm,
    wide_ref,
    narrow_ref,
    band_ref,
    pot_ref,
    speed_ref,
    sign_ref,
    band_sem,
    sems,
):
    count = pot_ref.shape[2] // 128
    pieces = count // blocks
    copies = [[] for _ in range(pieces)]
    band_copy = pltpu.make_async_copy(band_hbm, band_ref, band_sem)
    for i in range(pieces):
        here = slice(128 * blocks * i, 128 * blocks * (i + 1))
        for j, (source, target) in enumerate(
            ((pot_hbm, pot_ref), (sign_hbm, sign_ref), (speed_hbm, speed_ref))
        ):
            cut = (slice(None),) * (len(source.shape) - 1) + (here,)
            copies[i].append(
                pltpu.make_async_copy(source.at[cut], target.at[cut], sems.at[i, j])
            )
            copies[i][j].start()
        if i == 0:
            band_copy.start()
    band_copy.wait()
    copies[0][0].wait()
    band = stacked(band_ref[...], band_ref[...])

    def tall(value):
        return jnp.concatenate(
            [value[:, i : i + 128] for i in range(0, value.shape[1], 128)], axis=0
        )

    for first in range(0, count, blocks):
        i = first // blocks
        for copy in copies[i][1:] + [c[0] for c in copies[i + 1 : i + 2]]:
            copy.wait()
        start, stop = max(first - 1, 0), min(first + blocks + 1, count)
        around = slice(128 * start, 128 * stop)
        here = slice(128 * first, 128 * (first + blocks))
        value = tall(stacked(pot_ref[0, :, around], pot_ref[1, :, around]))
        zeros = jnp.zeros((8, 128), F32)
        if start == first:
            value = jnp.concatenate([zeros, value], axis=0)
        if stop == first + blocks:
            value = jnp.concatenate([value, zeros], axis=0)
        high, rest = split(value)
        both = jnp.concatenate([high.astype(BF16), rest.astype(BF16)], axis=1)
        parts = jnp.dot(both, band, preferred_element_type=F32)
        size = 8 * blocks
        mid, before, after = slice(8, 8 + size), slice(0, size), slice(16, 16 + size)
        total = parts[mid, :256] + parts[after, 256:512] + parts[before, 512:]
        sign = tall(stacked(sign_ref[0, :, here], sign_ref[1, :, here]).astype(F32))
        speed = tall(stacked(speed_ref[:, here], speed_ref[:, here]))
        swept = value[mid] - change_of(total[:, :128], total[:, 128:], sign, speed)
        swept = jnp.concatenate([swept[8 * i : 8 * i + 8] for i in range(blocks)], axis=1)
        wide_ref[:, here] = swept
        narrow_ref[:, here] = swept.astype(BF16)


def column_matrix():
    rows = np.zeros((2, 2, 7, 8, 64), np.float32)
    for odd in range(2):
        for section in range(2):
            part = rows[odd, section]
            for place in range(4):
                r = 3 - place if section else place
                for g in range(2):
                    at, own = 2 * place + g, 4 * g + r
                    for k in range(-4, 5):
                        block, source = divmod(r + k, 4)
                        if block == 0:
                            starts = (0, 8)
                        elif (block < 0) == bool(odd):
                            starts = (16, 24)
                        else:
                            starts = (32,)
                        for start in starts:
                            part[0, at, start + 4 * g + source] = CENTRAL[k + 4]
                            part[1, at, start + 4 * g + source] = BINOMIAL[k + 4]
                    part[2, at, [own, 8 + own]] = 1.0
                    part[3, at, 40 + own] = 1.0
                    part[4, at, [48 + r, 56 + r]] = 1.0
                    part[5, at, [52 + r, 60 + r]] = 1.0
                part[6, 4 + place, [52 + r, 60 + r]] = 1.0
    return rows.reshape(2, 2, 56, 64)


def sweep_y(
    size,
    column_ref,
    own_ref,
    chip_ref,
    far_ref,
    speed_ref,
    sign_ref,
    density_ref,
    own_rows_ref,
    inner_ref,
    outer_ref,
    swap_ref,
    edge_ref,
    cross_ref,
):
    columns = column_ref[lax.rem(lax.axis_index("wide"), 2), lax.axis_index("section")]
    row = lax.broadcasted_iota(jnp.int32, (8, size), 0)
    for start in range(0, own_ref.shape[1], size):
        here = slice(start, start + size)
        sign = stacked(sign_ref[0, :, here], sign_ref[1, :, here]).astype(F32)
        sources = (
            split(own_ref[:, here])
            + split(chip_ref[:, here])
            + (far_ref[:, here].astype(F32), sign)
            + split(stacked(speed_ref[:, here], density_ref[:, here]))
        )
        sources = jnp.concatenate(
            [stacked(sources[i], sources[i + 1]).astype(BF16) for i in range(0, 8, 2)], axis=0
        )
        parts = jnp.dot(columns, sources, preferred_element_type=F32)
        central, damping, own, sign, speed, density, crowd = (
            parts[8 * i : 8 * i + 8] for i in range(7)
        )
        physics = own - change_of(central, damping, sign, speed) + TIME_STEP * density
        turned = pltpu.roll(physics, 2, axis=0)
        own_rows_ref[:, here] = physics[0:4]
        inner_ref[:, here] = stacked(physics, crowd).astype(BF16)
        outer_ref[:, here] = stacked(turned, crowd).astype(BF16)
        narrow = physics.astype(BF16)
        for j in range(3):
            swap_ref[j, :, here] = narrow[2 * j + 2 : 2 * j + 4]
        edge = jnp.where(row < 2, turned, pltpu.roll(crowd, 3, axis=0))
        edge_ref[:, here] = edge[0:4].astype(BF16)
        cross_ref[:, here] = narrow[0:2]


def mix_features(size, start, length, features, mix_ref, fix_ref):
    value = features[:, start : start + size + 2 * HALO]
    patches = jnp.concatenate(
        [value[:, HALO + k : HALO + k + size] for k in range(-2, 3)], axis=0
    )
    mixed = jnp.dot(mix_ref[...], patches, preferred_element_type=F32)
    change = mixed[128:132] + mixed[132:136]
    mixed = mixed[:128]
    lane = lax.broadcasted_iota(jnp.int32, (16, HALO), 1)

    def at_rim(side, place, columns):
        column = jnp.where(lane == place, columns.astype(F32), 0.0).astype(BF16)
        return jnp.dot(fix_ref[side], column, preferred_element_type=F32)

    if start == 0:
        head = mixed[:, :HALO] - at_rim(0, 0, value[:, HALO : 2 * HALO])
        mixed = jnp.concatenate([head, mixed[:, HALO:]], axis=1)
    if start + size == length:
        tail = mixed[:, size - HALO :] - at_rim(1, HALO - 1, value[:, size : size + HALO])
        mixed = jnp.concatenate([mixed[:, : size - HALO], tail], axis=1)
    return mixed, change


def normalise(mixed):
    square = jnp.sum(mixed * mixed, axis=0, keepdims=True)
    inverse = lax.rsqrt(square * (1.0 / 128.0) + EPSILON)
    return (mixed * inverse).astype(BF16)


def lift_scaled(normed, up_ref):
    lift = jnp.dot(up_ref[...], normed, preferred_element_type=F32).astype(BF16)
    return lift + lift * jnp.tanh(lift * (lift * lift + BF16(GELU_LINEAR / GELU_SCALE)))


def correct(size, length, features, weight_refs, finish):
    mix_ref, fix_ref, up_ref, down_ref = weight_refs
    count = length // size
    mixed, normed, lifted, changes = {}, {}, {}, {}
    for t in range(count + 3 * LAG):
        if t < count:
            mixed[t], changes[t] = mix_features(
                size, t * size, length, features, mix_ref, fix_ref
            )
        u = t - 3 * LAG
        if u >= 0:
            result = jnp.dot(down_ref[...], lifted.pop(u), preferred_element_type=F32)
            finish(slice(u * size, u * size + size), changes.pop(u) + (result[0:4] + result[4:8]))
        u = t - 2 * LAG
        if 0 <= u < count:
            lifted[u] = lift_scaled(normed.pop(u), up_ref)
        u = t - LAG
        if 0 <= u < count:
            normed[u] = normalise(mixed.pop(u))


def in_groups(low, own, other):
    other = other.astype(F32)
    return jnp.where(
        low, jnp.concatenate([own, other], axis=0), jnp.concatenate([other, own], axis=0)
    )


def clear_rims(features, length):
    features[:, :HALO] = jnp.zeros((16, HALO), BF16)
    features[:, HALO + length :] = jnp.zeros((16, HALO), BF16)


def correct_inner(size, inner_ref, swap_ref, own_rows_ref, *refs):
    *weight_refs, out_ref, features = refs
    length = inner_ref.shape[1]
    low = lax.axis_index("section") == 0
    mid = slice(HALO, HALO + length)
    clear_rims(features, length)
    features[:, mid] = inner_ref[...]
    for j in range(3):
        features[6 + 2 * j : 8 + 2 * j, mid] = swap_ref[2 - j]

    def finish(here, change):
        own = own_rows_ref[2:4, here]
        out_ref[:, here] = change + in_groups(low, own, swap_ref[1, :, here])

    correct(size, length, features, weight_refs, finish)


def correct_outer(
    size, outer_ref, swap_ref, edge_ref, cross_ref, own_rows_ref, row_ref, *refs
):
    *weight_refs, out_hbm, features, out_ref, sems = refs
    length = outer_ref.shape[1]
    part = length // sems.shape[0]
    copies = []
    low = lax.axis_index("section") == 0
    mid = slice(HALO, HALO + length)
    clear_rims(features, length)
    features[:, mid] = outer_ref[...]
    features[0:2, mid] = edge_ref[0:2]
    features[14:16, mid] = edge_ref[2:4]
    features[6:8, mid] = cross_ref[...]
    features[10:12, mid] = swap_ref[1]

    features[8:10, mid] = swap_ref[2]

    def finish(here, change):
        outer_row = change + in_groups(low, own_rows_ref[0:2, here], swap_ref[2, :, here])
        inner_row = row_ref[:, here]
        out_ref[:, 0, here] = jnp.where(low, outer_row, inner_row)
        out_ref[:, 1, here] = jnp.where(low, inner_row, outer_row)
        if here.stop % part == 0:
            cut = (slice(None), slice(None), slice(here.stop - part, here.stop))
            copies.append(
                pltpu.make_async_copy(out_ref.at[cut], out_hbm.at[cut], sems.at[len(copies)])
            )
            copies[-1].start()

    correct(size, length, features, weight_refs, finish)
    for copy in copies:
        copy.wait()


def selections():
    picks = np.zeros((2, 2, 6, 45, 128), np.float32)
    for section in range(2):
        for outer in range(2):
            places = []
            for row in range(3):
                for group in range(4):
                    other = int(group // 2 != section)
                    shift = 2 - row if section else row
                    places.append((6 * other + 2 * row + group % 2, shift, group))
                crowd = 12 + ((row + 2) % 3 if outer else row)
                places.append((crowd, shift, 4))
            for place, shift, channel in places:
                for column in range(3):
                    source = 15 * shift + 5 * column + channel
                    for tap in range(3):
                        picks[section, outer, tap, source, 16 * (tap + column) + place] = 1.0
                    picks[section, outer, 3, source, 16 * (column + 1) + place] = 1.0
                picks[section, outer, 4, 15 * shift + 10 + channel, place] = 1.0
                picks[section, outer, 5, 15 * shift + channel, place] = 1.0
    return picks.transpose(0, 1, 3, 2, 4).reshape(2, 2, 45, 768)


def prepare(pick_ref, stem_ref, conv_ref, gain_ref, up_ref, down_ref, out_ref, *refs):
    inner_refs, outer_refs, (up_out, down_out) = refs[0:2], refs[2:4], refs[4:6]
    section = lax.axis_index("section")

    def turned(left, right):
        return lax.dot_general(
            left, right, (((0,), (0,)), ((), ())), preferred_element_type=F32
        )

    def unit(size):
        rows = lax.broadcasted_iota(jnp.int32, (size, size), 0)
        return jnp.where(rows == lax.broadcasted_iota(jnp.int32, (size, size), 1), 1.0, 0.0)

    conv = turned(conv_ref[0], unit(3).astype(BF16))
    for outer, (mix_out, fix_out) in enumerate((inner_refs, outer_refs)):
        picked = turned(stem_ref[...], pick_ref[section, outer])
        parts = [picked[:, 128 * i : 128 * i + 128] for i in range(6)]
        mix = sum(conv[:, i : i + 1] * parts[i] for i in range(3))
        direct = turned(out_ref[...], parts[3].astype(BF16))
        rows = jnp.concatenate([mix, direct, direct - direct.astype(BF16).astype(F32)], axis=0)
        mix_out[...] = rows[:, :80].astype(BF16)
        fix_out[0] = (conv[:, 0:1] * parts[4])[:, :16].astype(BF16)
        fix_out[1] = (conv[:, 2:3] * parts[5])[:, :16].astype(BF16)
    up = turned(up_ref[0], unit(128).astype(BF16))
    up_out[...] = (up * (GELU_SCALE * gain_ref[...])).astype(BF16)
    down = lax.dot_general(
        out_ref[...], down_ref[0], (((0,), (1,)), ((), ())), preferred_element_type=F32
    )
    down = (0.5 / GELU_SCALE) * down
    down_out[...] = jnp.concatenate([down, down - down.astype(BF16).astype(F32)], axis=0).astype(BF16)


def shards(
    potential,
    speed_x,
    speed_y,
    density,
    sign_x,
    sign_y,
    stem_weight,
    conv_weight,
    norm_gain,
    up_weight,
    down_weight,
    out_weight,
):
    length = potential.shape[2]
    size = min(length, 2048)
    chunk = min(length, 512)
    blocks = lax.axis_size("wide")
    shape = jax.ShapeDtypeStruct

    def swaps(first):
        pairs = [(2 * w + s, 2 * w + 2 + s) for w in range(first, blocks - 1, 2) for s in (0, 1)]
        return pairs + [(b, a) for a, b in pairs]

    swept, narrow = pl.pallas_call(
        functools.partial(sweep_x, length // 128),
        in_specs=[pl.BlockSpec(memory_space=pltpu.HBM)] * 4,
        out_shape=(shape((8, length), F32), shape((8, length), BF16)),
        scratch_shapes=[
            pltpu.VMEM((128, 768), BF16),
            pltpu.VMEM((2, 4, length), F32),
            pltpu.VMEM((4, length), F32),
            pltpu.VMEM((2, 4, length), jnp.int32),
            pltpu.SemaphoreType.DMA,
            pltpu.SemaphoreType.DMA((1, 3)),
        ],
        compiler_params=params(),
        name="sweep_x",
    )(
        *(
            pltpu.with_memory_space_constraint(value, pltpu.HBM)
            for value in (jnp.asarray(band_matrix(), BF16), potential, speed_x, sign_x)
        )
    )
    far = lax.ppermute(narrow, BOTH, swaps(1))
    chip = lax.ppermute(swept, BOTH, swaps(0))
    mix_shapes = (shape((136, 80), BF16), shape((2, 128, 16), BF16))
    shared_shapes = (shape((256, 128), BF16), shape((8, 256), BF16))
    made = pl.pallas_call(
        prepare,
        out_shape=mix_shapes + mix_shapes + shared_shapes,
        compiler_params=params(),
        name="prepare",
    )(
        jnp.asarray(selections(), BF16),
        stem_weight,
        conv_weight,
        norm_gain,
        up_weight,
        down_weight,
        out_weight,
    )
    chip, far, made = lax.optimization_barrier((chip, far, made))
    own_rows, inner, outer, given, edge, cross = pl.pallas_call(
        functools.partial(sweep_y, size),
        out_shape=(
            shape((4, length), F32),
            shape((16, length), BF16),
            shape((16, length), BF16),
            shape((3, 2, length), BF16),
            shape((4, length), BF16),
            shape((2, length), BF16),
        ),
        compiler_params=params(),
        name="sweep_y",
    )(jnp.asarray(column_matrix(), BF16), swept, chip, far, speed_y, sign_y, density)
    swap = lax.ppermute(given, "section", [(0, 1), (1, 0)])
    edge = lax.ppermute(
        edge,
        BOTH,
        [(2 * w + 1, 2 * w - 1) for w in range(1, blocks)]
        + [(2 * w, 2 * w + 2) for w in range(blocks - 1)],
    )
    cross = lax.ppermute(
        cross,
        BOTH,
        [(2 * w, 2 * w - 1) for w in range(1, blocks)]
        + [(2 * w + 1, 2 * w + 2) for w in range(blocks - 1)],
    )
    inner_weights, outer_weights = made[0:2] + made[4:6], made[2:6]
    scratch = [pltpu.VMEM((16, length + 2 * HALO), BF16)]
    row = pl.pallas_call(
        functools.partial(correct_inner, chunk),
        out_shape=shape((4, length), F32),
        scratch_shapes=scratch,
        compiler_params=params(),
        name="correct_inner",
    )(inner, swap, own_rows, *inner_weights)
    return pl.pallas_call(
        functools.partial(correct_outer, chunk),
        out_shape=shape((4, 2, length), F32),
        out_specs=pl.BlockSpec(memory_space=pltpu.HBM),
        scratch_shapes=scratch
        + [pltpu.VMEM((4, 2, length), F32), pltpu.SemaphoreType.DMA((min(8, length // chunk),))],
        compiler_params=params(),
        name="correct_outer",
    )(outer, swap, edge, cross, own_rows, row, *outer_weights)


def solution(mesh):
    placed = (
        P("section", "wide", None),
        P("wide", None),
        P("wide", None),
        P("wide", None),
        P("section", "wide", None),
        P("section", "wide", None),
        P(),
        P(),
        P(),
        P(),
        P(),
        P(),
    )
    return jax.shard_map(
        shards,
        mesh=mesh,
        in_specs=placed,
        out_specs=P(None, ("wide", "section"), None),
        check_vma=False,
    )
```

```python
import functools

import jax
import jax.numpy as jnp
import numpy as np
from jax import lax
from jax.experimental import pallas as pl
from jax.experimental.pallas import tpu as pltpu
from jax.sharding import PartitionSpec as P

CENTRAL = (3.0, -32.0, 168.0, -672.0, 0.0, 672.0, -168.0, 32.0, -3.0)
BINOMIAL = (1.0, -8.0, 28.0, -56.0, 70.0, -56.0, 28.0, -8.0, 1.0)
CENTRAL_UNIT = 1.0 / 840.0
DAMPING = 1.0 / 630.0
TIME_STEP = 0.6
EPSILON = 1e-06
GELU_LINEAR = 0.7978845608028654
GELU_SCALE = (GELU_LINEAR * 0.044715) ** (1.0 / 3.0)
BF16 = jnp.bfloat16
F32 = jnp.float32
BOTH = ("wide", "section")
HALO = 128
LAG = 2


def params(mebibytes=24):
    return pltpu.CompilerParams(vmem_limit_bytes=mebibytes << 20)


def stacked(first, second):
    return jnp.concatenate([first, second], axis=0)


def split(value):
    high = value.astype(BF16).astype(F32)
    return high, value - high


def change_of(central, damping, signs, speeds):
    gradient = CENTRAL_UNIT * central + ((2.0 * DAMPING) * signs - DAMPING) * damping
    return (TIME_STEP * speeds) * gradient


def band_matrix():
    bands = np.zeros((3, 128, 3, 2, 128), np.float32)
    for column in range(128):
        for k in range(-4, 5):
            block, lane = divmod(column + k, 128)
            bands[0, lane, block, 0, column] = CENTRAL[k + 4]
            bands[0, lane, block, 1, column] = BINOMIAL[k + 4]
    return bands[0].reshape(128, 768)


def sweep_x(
    blocks,
    band_hbm,
    pot_hbm,
    speed_hbm,
    sign_hbm,
    wide_ref,
    narrow_ref,
    band_ref,
    pot_ref,
    speed_ref,
    sign_ref,
    band_sem,
    sems,
):
    count = pot_ref.shape[2] // 128
    pieces = count // blocks
    copies = [[] for _ in range(pieces)]
    band_copy = pltpu.make_async_copy(band_hbm, band_ref, band_sem)
    for i in range(pieces):
        here = slice(128 * blocks * i, 128 * blocks * (i + 1))
        for j, (source, target) in enumerate(
            ((pot_hbm, pot_ref), (sign_hbm, sign_ref), (speed_hbm, speed_ref))
        ):
            cut = (slice(None),) * (len(source.shape) - 1) + (here,)
            copies[i].append(
                pltpu.make_async_copy(source.at[cut], target.at[cut], sems.at[i, j])
            )
            copies[i][j].start()
        if i == 0:
            band_copy.start()
    band_copy.wait()
    copies[0][0].wait()
    band = stacked(band_ref[...], band_ref[...])

    def tall(value):
        return jnp.concatenate(
            [value[:, i : i + 128] for i in range(0, value.shape[1], 128)], axis=0
        )

    for first in range(0, count, blocks):
        i = first // blocks
        for copy in copies[i][1:] + [c[0] for c in copies[i + 1 : i + 2]]:
            copy.wait()
        start, stop = max(first - 1, 0), min(first + blocks + 1, count)
        around = slice(128 * start, 128 * stop)
        here = slice(128 * first, 128 * (first + blocks))
        value = tall(stacked(pot_ref[0, :, around], pot_ref[1, :, around]))
        zeros = jnp.zeros((8, 128), F32)
        if start == first:
            value = jnp.concatenate([zeros, value], axis=0)
        if stop == first + blocks:
            value = jnp.concatenate([value, zeros], axis=0)
        high, rest = split(value)
        both = jnp.concatenate([high.astype(BF16), rest.astype(BF16)], axis=1)
        parts = jnp.dot(both, band, preferred_element_type=F32)
        size = 8 * blocks
        mid, before, after = slice(8, 8 + size), slice(0, size), slice(16, 16 + size)
        total = parts[mid, :256] + parts[after, 256:512] + parts[before, 512:]
        sign = tall(stacked(sign_ref[0, :, here], sign_ref[1, :, here]).astype(F32))
        speed = tall(stacked(speed_ref[:, here], speed_ref[:, here]))
        swept = value[mid] - change_of(total[:, :128], total[:, 128:], sign, speed)
        swept = jnp.concatenate([swept[8 * i : 8 * i + 8] for i in range(blocks)], axis=1)
        wide_ref[:, here] = swept
        narrow_ref[:, here] = swept.astype(BF16)


def column_matrix():
    rows = np.zeros((2, 2, 7, 8, 64), np.float32)
    for odd in range(2):
        for section in range(2):
            part = rows[odd, section]
            for place in range(4):
                r = 3 - place if section else place
                for g in range(2):
                    at, own = 2 * place + g, 4 * g + r
                    for k in range(-4, 5):
                        block, source = divmod(r + k, 4)
                        if block == 0:
                            starts = (0, 8)
                        elif (block < 0) == bool(odd):
                            starts = (16, 24)
                        else:
                            starts = (32,)
                        for start in starts:
                            part[0, at, start + 4 * g + source] = CENTRAL[k + 4]
                            part[1, at, start + 4 * g + source] = BINOMIAL[k + 4]
                    part[2, at, [own, 8 + own]] = 1.0
                    part[3, at, 40 + own] = 1.0
                    part[4, at, [48 + r, 56 + r]] = 1.0
                    part[5, at, [52 + r, 60 + r]] = 1.0
                part[6, 4 + place, [52 + r, 60 + r]] = 1.0
    return rows.reshape(2, 2, 56, 64)


def sweep_y(
    size,
    column_ref,
    own_ref,
    chip_ref,
    far_ref,
    speed_ref,
    sign_ref,
    density_ref,
    own_rows_ref,
    inner_ref,
    outer_ref,
    swap_ref,
    edge_ref,
    cross_ref,
):
    columns = column_ref[lax.rem(lax.axis_index("wide"), 2), lax.axis_index("section")]
    row = lax.broadcasted_iota(jnp.int32, (8, size), 0)
    for start in range(0, own_ref.shape[1], size):
        here = slice(start, start + size)
        sign = stacked(sign_ref[0, :, here], sign_ref[1, :, here]).astype(F32)
        sources = (
            split(own_ref[:, here])
            + split(chip_ref[:, here])
            + (far_ref[:, here].astype(F32), sign)
            + split(stacked(speed_ref[:, here], density_ref[:, here]))
        )
        sources = jnp.concatenate(
            [stacked(sources[i], sources[i + 1]).astype(BF16) for i in range(0, 8, 2)], axis=0
        )
        parts = jnp.dot(columns, sources, preferred_element_type=F32)
        central, damping, own, sign, speed, density, crowd = (
            parts[8 * i : 8 * i + 8] for i in range(7)
        )
        physics = own - change_of(central, damping, sign, speed) + TIME_STEP * density
        turned = pltpu.roll(physics, 2, axis=0)
        own_rows_ref[:, here] = physics[0:4]
        inner_ref[:, here] = stacked(physics, crowd).astype(BF16)
        outer_ref[:, here] = stacked(turned, crowd).astype(BF16)
        narrow = physics.astype(BF16)
        for j in range(3):
            swap_ref[j, :, here] = narrow[2 * j + 2 : 2 * j + 4]
        edge = jnp.where(row < 2, turned, pltpu.roll(crowd, 3, axis=0))
        edge_ref[:, here] = edge[0:4].astype(BF16)
        cross_ref[:, here] = narrow[0:2]


def mix_features(size, start, length, features, mix_ref, fix_ref):
    value = features[:, start : start + size + 2 * HALO]
    patches = jnp.concatenate(
        [value[:, HALO + k : HALO + k + size] for k in range(-2, 3)], axis=0
    )
    mixed = jnp.dot(mix_ref[...], patches, preferred_element_type=F32)
    change = mixed[128:132] + mixed[132:136]
    mixed = mixed[:128]
    lane = lax.broadcasted_iota(jnp.int32, (16, HALO), 1)

    def at_rim(side, place, columns):
        column = jnp.where(lane == place, columns.astype(F32), 0.0).astype(BF16)
        return jnp.dot(fix_ref[side], column, preferred_element_type=F32)

    if start == 0:
        head = mixed[:, :HALO] - at_rim(0, 0, value[:, HALO : 2 * HALO])
        mixed = jnp.concatenate([head, mixed[:, HALO:]], axis=1)
    if start + size == length:
        tail = mixed[:, size - HALO :] - at_rim(1, HALO - 1, value[:, size : size + HALO])
        mixed = jnp.concatenate([mixed[:, : size - HALO], tail], axis=1)
    return mixed, change


def normalise(mixed):
    square = jnp.sum(mixed * mixed, axis=0, keepdims=True)
    inverse = lax.rsqrt(square * (1.0 / 128.0) + EPSILON)
    return (mixed * inverse).astype(BF16)


def lift_scaled(normed, up_ref):
    lift = jnp.dot(up_ref[...], normed, preferred_element_type=F32).astype(BF16)
    return lift + lift * jnp.tanh(lift * (lift * lift + BF16(GELU_LINEAR / GELU_SCALE)))


def correct(size, length, features, weight_refs, finish):
    mix_ref, fix_ref, up_ref, down_ref = weight_refs
    count = length // size
    mixed, normed, lifted, changes = {}, {}, {}, {}
    for t in range(count + 3 * LAG):
        if t < count:
            mixed[t], changes[t] = mix_features(
                size, t * size, length, features, mix_ref, fix_ref
            )
        u = t - 3 * LAG
        if u >= 0:
            result = jnp.dot(down_ref[...], lifted.pop(u), preferred_element_type=F32)
            finish(slice(u * size, u * size + size), changes.pop(u) + (result[0:4] + result[4:8]))
        u = t - 2 * LAG
        if 0 <= u < count:
            lifted[u] = lift_scaled(normed.pop(u), up_ref)
        u = t - LAG
        if 0 <= u < count:
            normed[u] = normalise(mixed.pop(u))


def in_groups(low, own, other):
    other = other.astype(F32)
    return jnp.where(
        low, jnp.concatenate([own, other], axis=0), jnp.concatenate([other, own], axis=0)
    )


def clear_rims(features, length):
    features[:, :HALO] = jnp.zeros((16, HALO), BF16)
    features[:, HALO + length :] = jnp.zeros((16, HALO), BF16)


def correct_inner(size, inner_ref, swap_ref, own_rows_ref, *refs):
    *weight_refs, out_ref, features = refs
    length = inner_ref.shape[1]
    low = lax.axis_index("section") == 0
    mid = slice(HALO, HALO + length)
    clear_rims(features, length)
    features[:, mid] = inner_ref[...]
    for j in range(3):
        features[6 + 2 * j : 8 + 2 * j, mid] = swap_ref[2 - j]

    def finish(here, change):
        own = own_rows_ref[2:4, here]
        out_ref[:, here] = change + in_groups(low, own, swap_ref[1, :, here])

    correct(size, length, features, weight_refs, finish)


def correct_outer(
    size, outer_ref, swap_ref, edge_ref, cross_ref, own_rows_ref, row_ref, *refs
):
    *weight_refs, out_hbm, features, out_ref, sems = refs
    length = outer_ref.shape[1]
    part = length // sems.shape[0]
    copies = []
    low = lax.axis_index("section") == 0
    mid = slice(HALO, HALO + length)
    clear_rims(features, length)
    features[:, mid] = outer_ref[...]
    features[0:2, mid] = edge_ref[0:2]
    features[14:16, mid] = edge_ref[2:4]
    features[6:8, mid] = cross_ref[...]
    features[10:12, mid] = swap_ref[1]

    features[8:10, mid] = swap_ref[2]

    def finish(here, change):
        outer_row = change + in_groups(low, own_rows_ref[0:2, here], swap_ref[2, :, here])
        inner_row = row_ref[:, here]
        out_ref[:, 0, here] = jnp.where(low, outer_row, inner_row)
        out_ref[:, 1, here] = jnp.where(low, inner_row, outer_row)
        if here.stop % part == 0:
            cut = (slice(None), slice(None), slice(here.stop - part, here.stop))
            copies.append(
                pltpu.make_async_copy(out_ref.at[cut], out_hbm.at[cut], sems.at[len(copies)])
            )
            copies[-1].start()

    correct(size, length, features, weight_refs, finish)
    for copy in copies:
        copy.wait()


def selections():
    picks = np.zeros((2, 2, 6, 45, 128), np.float32)
    for section in range(2):
        for outer in range(2):
            places = []
            for row in range(3):
                for group in range(4):
                    other = int(group // 2 != section)
                    shift = 2 - row if section else row
                    places.append((6 * other + 2 * row + group % 2, shift, group))
                crowd = 12 + ((row + 2) % 3 if outer else row)
                places.append((crowd, shift, 4))
            for place, shift, channel in places:
                for column in range(3):
                    source = 15 * shift + 5 * column + channel
                    for tap in range(3):
                        picks[section, outer, tap, source, 16 * (tap + column) + place] = 1.0
                    picks[section, outer, 3, source, 16 * (column + 1) + place] = 1.0
                picks[section, outer, 4, 15 * shift + 10 + channel, place] = 1.0
                picks[section, outer, 5, 15 * shift + channel, place] = 1.0
    return picks.transpose(0, 1, 3, 2, 4).reshape(2, 2, 45, 768)


def prepare(pick_ref, stem_ref, conv_ref, gain_ref, up_ref, down_ref, out_ref, *refs):
    inner_refs, outer_refs, (up_out, down_out) = refs[0:2], refs[2:4], refs[4:6]
    section = lax.axis_index("section")

    def turned(left, right):
        return lax.dot_general(
            left, right, (((0,), (0,)), ((), ())), preferred_element_type=F32
        )

    def unit(size):
        rows = lax.broadcasted_iota(jnp.int32, (size, size), 0)
        return jnp.where(rows == lax.broadcasted_iota(jnp.int32, (size, size), 1), 1.0, 0.0)

    conv = turned(conv_ref[0], unit(3).astype(BF16))
    for outer, (mix_out, fix_out) in enumerate((inner_refs, outer_refs)):
        picked = turned(stem_ref[...], pick_ref[section, outer])
        parts = [picked[:, 128 * i : 128 * i + 128] for i in range(6)]
        mix = sum(conv[:, i : i + 1] * parts[i] for i in range(3))
        direct = turned(out_ref[...], parts[3].astype(BF16))
        rows = jnp.concatenate([mix, direct, direct - direct.astype(BF16).astype(F32)], axis=0)
        mix_out[...] = rows[:, :80].astype(BF16)
        fix_out[0] = (conv[:, 0:1] * parts[4])[:, :16].astype(BF16)
        fix_out[1] = (conv[:, 2:3] * parts[5])[:, :16].astype(BF16)
    up = turned(up_ref[0], unit(128).astype(BF16))
    up_out[...] = (up * (GELU_SCALE * gain_ref[...])).astype(BF16)
    down = lax.dot_general(
        out_ref[...], down_ref[0], (((0,), (1,)), ((), ())), preferred_element_type=F32
    )
    down = (0.5 / GELU_SCALE) * down
    down_out[...] = jnp.concatenate([down, down - down.astype(BF16).astype(F32)], axis=0).astype(BF16)


def shards(
    potential,
    speed_x,
    speed_y,
    density,
    sign_x,
    sign_y,
    stem_weight,
    conv_weight,
    norm_gain,
    up_weight,
    down_weight,
    out_weight,
):
    length = potential.shape[2]
    size = min(length, 2048)
    chunk = min(length, 1024)
    blocks = lax.axis_size("wide")
    shape = jax.ShapeDtypeStruct

    def swaps(first):
        pairs = [(2 * w + s, 2 * w + 2 + s) for w in range(first, blocks - 1, 2) for s in (0, 1)]
        return pairs + [(b, a) for a, b in pairs]

    swept, narrow = pl.pallas_call(
        functools.partial(sweep_x, length // 128),
        in_specs=[pl.BlockSpec(memory_space=pltpu.HBM)] * 4,
        out_shape=(shape((8, length), F32), shape((8, length), BF16)),
        scratch_shapes=[
            pltpu.VMEM((128, 768), BF16),
            pltpu.VMEM((2, 4, length), F32),
            pltpu.VMEM((4, length), F32),
            pltpu.VMEM((2, 4, length), jnp.int32),
            pltpu.SemaphoreType.DMA,
            pltpu.SemaphoreType.DMA((1, 3)),
        ],
        compiler_params=params(),
        name="sweep_x",
    )(
        *(
            pltpu.with_memory_space_constraint(value, pltpu.HBM)
            for value in (jnp.asarray(band_matrix(), BF16), potential, speed_x, sign_x)
        )
    )
    far = lax.ppermute(narrow, BOTH, swaps(1))
    chip = lax.ppermute(swept, BOTH, swaps(0))
    mix_shapes = (shape((136, 80), BF16), shape((2, 128, 16), BF16))
    shared_shapes = (shape((256, 128), BF16), shape((8, 256), BF16))
    made = pl.pallas_call(
        prepare,
        out_shape=mix_shapes + mix_shapes + shared_shapes,
        compiler_params=params(),
        name="prepare",
    )(
        jnp.asarray(selections(), BF16),
        stem_weight,
        conv_weight,
        norm_gain,
        up_weight,
        down_weight,
        out_weight,
    )
    chip, far, made = lax.optimization_barrier((chip, far, made))
    own_rows, inner, outer, given, edge, cross = pl.pallas_call(
        functools.partial(sweep_y, size),
        out_shape=(
            shape((4, length), F32),
            shape((16, length), BF16),
            shape((16, length), BF16),
            shape((3, 2, length), BF16),
            shape((4, length), BF16),
            shape((2, length), BF16),
        ),
        compiler_params=params(),
        name="sweep_y",
    )(jnp.asarray(column_matrix(), BF16), swept, chip, far, speed_y, sign_y, density)
    swap = lax.ppermute(given, "section", [(0, 1), (1, 0)])
    edge = lax.ppermute(
        edge,
        BOTH,
        [(2 * w + 1, 2 * w - 1) for w in range(1, blocks)]
        + [(2 * w, 2 * w + 2) for w in range(blocks - 1)],
    )
    cross = lax.ppermute(
        cross,
        BOTH,
        [(2 * w, 2 * w - 1) for w in range(1, blocks)]
        + [(2 * w + 1, 2 * w + 2) for w in range(blocks - 1)],
    )
    inner_weights, outer_weights = made[0:2] + made[4:6], made[2:6]
    scratch = [pltpu.VMEM((16, length + 2 * HALO), BF16)]
    row = pl.pallas_call(
        functools.partial(correct_inner, chunk),
        out_shape=shape((4, length), F32),
        scratch_shapes=scratch,
        compiler_params=params(),
        name="correct_inner",
    )(inner, swap, own_rows, *inner_weights)
    return pl.pallas_call(
        functools.partial(correct_outer, chunk),
        out_shape=shape((4, 2, length), F32),
        out_specs=pl.BlockSpec(memory_space=pltpu.HBM),
        scratch_shapes=scratch
        + [pltpu.VMEM((4, 2, length), F32), pltpu.SemaphoreType.DMA((min(8, length // chunk),))],
        compiler_params=params(),
        name="correct_outer",
    )(outer, swap, edge, cross, own_rows, row, *outer_weights)


def solution(mesh):
    placed = (
        P("section", "wide", None),
        P("wide", None),
        P("wide", None),
        P("wide", None),
        P("section", "wide", None),
        P("section", "wide", None),
        P(),
        P(),
        P(),
        P(),
        P(),
        P(),
    )
    return jax.shard_map(
        shards,
        mesh=mesh,
        in_specs=placed,
        out_specs=P(None, ("wide", "section"), None),
        check_vma=False,
    )
```

```python
import functools

import jax
import jax.numpy as jnp
import numpy as np
from jax import lax
from jax.experimental import pallas as pl
from jax.experimental.pallas import tpu as pltpu
from jax.sharding import PartitionSpec as P

CENTRAL = (3.0, -32.0, 168.0, -672.0, 0.0, 672.0, -168.0, 32.0, -3.0)
BINOMIAL = (1.0, -8.0, 28.0, -56.0, 70.0, -56.0, 28.0, -8.0, 1.0)
CENTRAL_UNIT = 1.0 / 840.0
DAMPING = 1.0 / 630.0
TIME_STEP = 0.6
EPSILON = 1e-06
GELU_LINEAR = 0.7978845608028654
GELU_SCALE = (GELU_LINEAR * 0.044715) ** (1.0 / 3.0)
BF16 = jnp.bfloat16
F32 = jnp.float32
BOTH = ("wide", "section")
HALO = 128
LAG = 2


def params(mebibytes=24):
    return pltpu.CompilerParams(vmem_limit_bytes=mebibytes << 20)


def stacked(first, second):
    return jnp.concatenate([first, second], axis=0)


def split(value):
    high = value.astype(BF16).astype(F32)
    return high, value - high


def change_of(central, damping, signs, speeds):
    gradient = CENTRAL_UNIT * central + ((2.0 * DAMPING) * signs - DAMPING) * damping
    return (TIME_STEP * speeds) * gradient


def band_matrix():
    bands = np.zeros((3, 128, 3, 2, 128), np.float32)
    for column in range(128):
        for k in range(-4, 5):
            block, lane = divmod(column + k, 128)
            bands[0, lane, block, 0, column] = CENTRAL[k + 4]
            bands[0, lane, block, 1, column] = BINOMIAL[k + 4]
    return bands[0].reshape(128, 768)


def sweep_x(
    blocks,
    band_hbm,
    pot_hbm,
    speed_hbm,
    sign_hbm,
    wide_ref,
    narrow_ref,
    band_ref,
    pot_ref,
    speed_ref,
    sign_ref,
    band_sem,
    sems,
):
    count = pot_ref.shape[2] // 128
    pieces = count // blocks
    copies = [[] for _ in range(pieces)]
    band_copy = pltpu.make_async_copy(band_hbm, band_ref, band_sem)
    for i in range(pieces):
        here = slice(128 * blocks * i, 128 * blocks * (i + 1))
        for j, (source, target) in enumerate(
            ((pot_hbm, pot_ref), (sign_hbm, sign_ref), (speed_hbm, speed_ref))
        ):
            cut = (slice(None),) * (len(source.shape) - 1) + (here,)
            copies[i].append(
                pltpu.make_async_copy(source.at[cut], target.at[cut], sems.at[i, j])
            )
            copies[i][j].start()
        if i == 0:
            band_copy.start()
    band_copy.wait()
    copies[0][0].wait()
    band = stacked(band_ref[...], band_ref[...])

    def tall(value):
        return jnp.concatenate(
            [value[:, i : i + 128] for i in range(0, value.shape[1], 128)], axis=0
        )

    for first in range(0, count, blocks):
        i = first // blocks
        for copy in copies[i][1:] + [c[0] for c in copies[i + 1 : i + 2]]:
            copy.wait()
        start, stop = max(first - 1, 0), min(first + blocks + 1, count)
        around = slice(128 * start, 128 * stop)
        here = slice(128 * first, 128 * (first + blocks))
        value = tall(stacked(pot_ref[0, :, around], pot_ref[1, :, around]))
        zeros = jnp.zeros((8, 128), F32)
        if start == first:
            value = jnp.concatenate([zeros, value], axis=0)
        if stop == first + blocks:
            value = jnp.concatenate([value, zeros], axis=0)
        high, rest = split(value)
        both = jnp.concatenate([high.astype(BF16), rest.astype(BF16)], axis=1)
        parts = jnp.dot(both, band, preferred_element_type=F32)
        size = 8 * blocks
        mid, before, after = slice(8, 8 + size), slice(0, size), slice(16, 16 + size)
        total = parts[mid, :256] + parts[after, 256:512] + parts[before, 512:]
        sign = tall(stacked(sign_ref[0, :, here], sign_ref[1, :, here]).astype(F32))
        speed = tall(stacked(speed_ref[:, here], speed_ref[:, here]))
        swept = value[mid] - change_of(total[:, :128], total[:, 128:], sign, speed)
        swept = jnp.concatenate([swept[8 * i : 8 * i + 8] for i in range(blocks)], axis=1)
        wide_ref[:, here] = swept
        narrow_ref[:, here] = swept.astype(BF16)


def column_matrix():
    rows = np.zeros((2, 2, 7, 8, 64), np.float32)
    for odd in range(2):
        for section in range(2):
            part = rows[odd, section]
            for place in range(4):
                r = 3 - place if section else place
                for g in range(2):
                    at, own = 2 * place + g, 4 * g + r
                    for k in range(-4, 5):
                        block, source = divmod(r + k, 4)
                        if block == 0:
                            starts = (0, 8)
                        elif (block < 0) == bool(odd):
                            starts = (16, 24)
                        else:
                            starts = (32,)
                        for start in starts:
                            part[0, at, start + 4 * g + source] = CENTRAL[k + 4]
                            part[1, at, start + 4 * g + source] = BINOMIAL[k + 4]
                    part[2, at, [own, 8 + own]] = 1.0
                    part[3, at, 40 + own] = 1.0
                    part[4, at, [48 + r, 56 + r]] = 1.0
                    part[5, at, [52 + r, 60 + r]] = 1.0
                part[6, 4 + place, [52 + r, 60 + r]] = 1.0
    return rows.reshape(2, 2, 56, 64)


def sweep_y(
    size,
    column_ref,
    own_ref,
    chip_ref,
    far_ref,
    speed_ref,
    sign_ref,
    density_ref,
    own_rows_ref,
    inner_ref,
    outer_ref,
    swap_ref,
    edge_ref,
    cross_ref,
):
    columns = column_ref[lax.rem(lax.axis_index("wide"), 2), lax.axis_index("section")]
    row = lax.broadcasted_iota(jnp.int32, (8, size), 0)
    for start in range(0, own_ref.shape[1], size):
        here = slice(start, start + size)
        sign = stacked(sign_ref[0, :, here], sign_ref[1, :, here]).astype(F32)
        sources = (
            split(own_ref[:, here])
            + split(chip_ref[:, here])
            + (far_ref[:, here].astype(F32), sign)
            + split(stacked(speed_ref[:, here], density_ref[:, here]))
        )
        sources = jnp.concatenate(
            [stacked(sources[i], sources[i + 1]).astype(BF16) for i in range(0, 8, 2)], axis=0
        )
        parts = jnp.dot(columns, sources, preferred_element_type=F32)
        central, damping, own, sign, speed, density, crowd = (
            parts[8 * i : 8 * i + 8] for i in range(7)
        )
        physics = own - change_of(central, damping, sign, speed) + TIME_STEP * density
        turned = pltpu.roll(physics, 2, axis=0)
        own_rows_ref[:, here] = physics[0:4]
        inner_ref[:, here] = stacked(physics, crowd).astype(BF16)
        outer_ref[:, here] = stacked(turned, crowd).astype(BF16)
        narrow = physics.astype(BF16)
        for j in range(3):
            swap_ref[j, :, here] = narrow[2 * j + 2 : 2 * j + 4]
        edge = jnp.where(row < 2, turned, pltpu.roll(crowd, 3, axis=0))
        edge_ref[:, here] = edge[0:4].astype(BF16)
        cross_ref[:, here] = narrow[0:2]


def mix_features(size, start, length, features, mix_ref, fix_ref):
    value = features[:, start : start + size + 2 * HALO]
    patches = jnp.concatenate(
        [value[:, HALO + k : HALO + k + size] for k in range(-2, 3)], axis=0
    )
    mixed = jnp.dot(mix_ref[...], patches, preferred_element_type=F32)
    change = mixed[128:132] + mixed[132:136]
    mixed = mixed[:128]
    lane = lax.broadcasted_iota(jnp.int32, (16, HALO), 1)

    def at_rim(side, place, columns):
        column = jnp.where(lane == place, columns.astype(F32), 0.0).astype(BF16)
        return jnp.dot(fix_ref[side], column, preferred_element_type=F32)

    if start == 0:
        head = mixed[:, :HALO] - at_rim(0, 0, value[:, HALO : 2 * HALO])
        mixed = jnp.concatenate([head, mixed[:, HALO:]], axis=1)
    if start + size == length:
        tail = mixed[:, size - HALO :] - at_rim(1, HALO - 1, value[:, size : size + HALO])
        mixed = jnp.concatenate([mixed[:, : size - HALO], tail], axis=1)
    return mixed, change


def normalise(mixed):
    square = jnp.sum(mixed * mixed, axis=0, keepdims=True)
    inverse = lax.rsqrt(square * (1.0 / 128.0) + EPSILON)
    return (mixed * inverse).astype(BF16)


def lift_scaled(normed, up_ref):
    lift = jnp.dot(up_ref[...], normed, preferred_element_type=F32).astype(BF16)
    return lift + lift * jnp.tanh(lift * (lift * lift + BF16(GELU_LINEAR / GELU_SCALE)))


def correct(size, length, features, weight_refs, finish):
    mix_ref, fix_ref, up_ref, down_ref = weight_refs
    count = length // size
    mixed, normed, lifted, changes = {}, {}, {}, {}
    for t in range(count + 3 * LAG):
        if t < count:
            mixed[t], changes[t] = mix_features(
                size, t * size, length, features, mix_ref, fix_ref
            )
        u = t - 3 * LAG
        if u >= 0:
            result = jnp.dot(down_ref[...], lifted.pop(u), preferred_element_type=F32)
            finish(slice(u * size, u * size + size), changes.pop(u) + (result[0:4] + result[4:8]))
        u = t - 2 * LAG
        if 0 <= u < count:
            lifted[u] = lift_scaled(normed.pop(u), up_ref)
        u = t - LAG
        if 0 <= u < count:
            normed[u] = normalise(mixed.pop(u))


def in_groups(low, own, other):
    other = other.astype(F32)
    return jnp.where(
        low, jnp.concatenate([own, other], axis=0), jnp.concatenate([other, own], axis=0)
    )


def clear_rims(features, length):
    features[:, :HALO] = jnp.zeros((16, HALO), BF16)
    features[:, HALO + length :] = jnp.zeros((16, HALO), BF16)


def correct_inner(size, inner_ref, swap_ref, own_rows_ref, *refs):
    *weight_refs, out_ref, features = refs
    length = inner_ref.shape[1]
    low = lax.axis_index("section") == 0
    mid = slice(HALO, HALO + length)
    clear_rims(features, length)
    features[:, mid] = inner_ref[...]
    for j in range(3):
        features[6 + 2 * j : 8 + 2 * j, mid] = swap_ref[2 - j]

    def finish(here, change):
        own = own_rows_ref[2:4, here]
        out_ref[:, here] = change + in_groups(low, own, swap_ref[1, :, here])

    correct(size, length, features, weight_refs, finish)


def correct_outer(
    size, outer_ref, swap_ref, edge_ref, cross_ref, own_rows_ref, row_ref, *refs
):
    *weight_refs, out_hbm, features, out_ref, sems = refs
    length = outer_ref.shape[1]
    part = length // sems.shape[0]
    copies = []
    low = lax.axis_index("section") == 0
    mid = slice(HALO, HALO + length)
    clear_rims(features, length)
    features[:, mid] = outer_ref[...]
    features[0:2, mid] = edge_ref[0:2]
    features[14:16, mid] = edge_ref[2:4]
    features[6:8, mid] = cross_ref[...]
    features[10:12, mid] = swap_ref[1]

    features[8:10, mid] = swap_ref[2]

    def finish(here, change):
        outer_row = change + in_groups(low, own_rows_ref[0:2, here], swap_ref[2, :, here])
        inner_row = row_ref[:, here]
        out_ref[:, 0, here] = jnp.where(low, outer_row, inner_row)
        out_ref[:, 1, here] = jnp.where(low, inner_row, outer_row)
        if here.stop % part == 0:
            cut = (slice(None), slice(None), slice(here.stop - part, here.stop))
            copies.append(
                pltpu.make_async_copy(out_ref.at[cut], out_hbm.at[cut], sems.at[len(copies)])
            )
            copies[-1].start()

    correct(size, length, features, weight_refs, finish)
    for copy in copies:
        copy.wait()


def selections():
    picks = np.zeros((2, 2, 6, 45, 128), np.float32)
    for section in range(2):
        for outer in range(2):
            places = []
            for row in range(3):
                for group in range(4):
                    other = int(group // 2 != section)
                    shift = 2 - row if section else row
                    places.append((6 * other + 2 * row + group % 2, shift, group))
                crowd = 12 + ((row + 2) % 3 if outer else row)
                places.append((crowd, shift, 4))
            for place, shift, channel in places:
                for column in range(3):
                    source = 15 * shift + 5 * column + channel
                    for tap in range(3):
                        picks[section, outer, tap, source, 16 * (tap + column) + place] = 1.0
                    picks[section, outer, 3, source, 16 * (column + 1) + place] = 1.0
                picks[section, outer, 4, 15 * shift + 10 + channel, place] = 1.0
                picks[section, outer, 5, 15 * shift + channel, place] = 1.0
    return picks.transpose(0, 1, 3, 2, 4).reshape(2, 2, 45, 768)


def prepare(pick_ref, stem_ref, conv_ref, gain_ref, up_ref, down_ref, out_ref, *refs):
    inner_refs, outer_refs, (up_out, down_out) = refs[0:2], refs[2:4], refs[4:6]
    section = lax.axis_index("section")

    def turned(left, right):
        return lax.dot_general(
            left, right, (((0,), (0,)), ((), ())), preferred_element_type=F32
        )

    def unit(size):
        rows = lax.broadcasted_iota(jnp.int32, (size, size), 0)
        return jnp.where(rows == lax.broadcasted_iota(jnp.int32, (size, size), 1), 1.0, 0.0)

    conv = turned(conv_ref[0], unit(3).astype(BF16))
    for outer, (mix_out, fix_out) in enumerate((inner_refs, outer_refs)):
        picked = turned(stem_ref[...], pick_ref[section, outer])
        parts = [picked[:, 128 * i : 128 * i + 128] for i in range(6)]
        mix = sum(conv[:, i : i + 1] * parts[i] for i in range(3))
        direct = turned(out_ref[...], parts[3].astype(BF16))
        rows = jnp.concatenate([mix, direct, direct - direct.astype(BF16).astype(F32)], axis=0)
        mix_out[...] = rows[:, :80].astype(BF16)
        fix_out[0] = (conv[:, 0:1] * parts[4])[:, :16].astype(BF16)
        fix_out[1] = (conv[:, 2:3] * parts[5])[:, :16].astype(BF16)
    up = turned(up_ref[0], unit(128).astype(BF16))
    up_out[...] = (up * (GELU_SCALE * gain_ref[...])).astype(BF16)
    down = lax.dot_general(
        out_ref[...], down_ref[0], (((0,), (1,)), ((), ())), preferred_element_type=F32
    )
    down = (0.5 / GELU_SCALE) * down
    down_out[...] = jnp.concatenate([down, down - down.astype(BF16).astype(F32)], axis=0).astype(BF16)


def shards(
    potential,
    speed_x,
    speed_y,
    density,
    sign_x,
    sign_y,
    stem_weight,
    conv_weight,
    norm_gain,
    up_weight,
    down_weight,
    out_weight,
):
    length = potential.shape[2]
    size = min(length, 4096)
    chunk = min(length, 1024)
    blocks = lax.axis_size("wide")
    shape = jax.ShapeDtypeStruct

    def swaps(first):
        pairs = [(2 * w + s, 2 * w + 2 + s) for w in range(first, blocks - 1, 2) for s in (0, 1)]
        return pairs + [(b, a) for a, b in pairs]

    swept, narrow = pl.pallas_call(
        functools.partial(sweep_x, length // 128),
        in_specs=[pl.BlockSpec(memory_space=pltpu.HBM)] * 4,
        out_shape=(shape((8, length), F32), shape((8, length), BF16)),
        scratch_shapes=[
            pltpu.VMEM((128, 768), BF16),
            pltpu.VMEM((2, 4, length), F32),
            pltpu.VMEM((4, length), F32),
            pltpu.VMEM((2, 4, length), jnp.int32),
            pltpu.SemaphoreType.DMA,
            pltpu.SemaphoreType.DMA((1, 3)),
        ],
        compiler_params=params(),
        name="sweep_x",
    )(
        *(
            pltpu.with_memory_space_constraint(value, pltpu.HBM)
            for value in (jnp.asarray(band_matrix(), BF16), potential, speed_x, sign_x)
        )
    )
    far = lax.ppermute(narrow, BOTH, swaps(1))
    chip = lax.ppermute(swept, BOTH, swaps(0))
    mix_shapes = (shape((136, 80), BF16), shape((2, 128, 16), BF16))
    shared_shapes = (shape((256, 128), BF16), shape((8, 256), BF16))
    made = pl.pallas_call(
        prepare,
        out_shape=mix_shapes + mix_shapes + shared_shapes,
        compiler_params=params(),
        name="prepare",
    )(
        jnp.asarray(selections(), BF16),
        stem_weight,
        conv_weight,
        norm_gain,
        up_weight,
        down_weight,
        out_weight,
    )
    chip, far, made = lax.optimization_barrier((chip, far, made))
    own_rows, inner, outer, given, edge, cross = pl.pallas_call(
        functools.partial(sweep_y, size),
        out_shape=(
            shape((4, length), F32),
            shape((16, length), BF16),
            shape((16, length), BF16),
            shape((3, 2, length), BF16),
            shape((4, length), BF16),
            shape((2, length), BF16),
        ),
        compiler_params=params(),
        name="sweep_y",
    )(jnp.asarray(column_matrix(), BF16), swept, chip, far, speed_y, sign_y, density)
    swap = lax.ppermute(given, "section", [(0, 1), (1, 0)])
    edge = lax.ppermute(
        edge,
        BOTH,
        [(2 * w + 1, 2 * w - 1) for w in range(1, blocks)]
        + [(2 * w, 2 * w + 2) for w in range(blocks - 1)],
    )
    cross = lax.ppermute(
        cross,
        BOTH,
        [(2 * w, 2 * w - 1) for w in range(1, blocks)]
        + [(2 * w + 1, 2 * w + 2) for w in range(blocks - 1)],
    )
    inner_weights, outer_weights = made[0:2] + made[4:6], made[2:6]
    scratch = [pltpu.VMEM((16, length + 2 * HALO), BF16)]
    row = pl.pallas_call(
        functools.partial(correct_inner, chunk),
        out_shape=shape((4, length), F32),
        scratch_shapes=scratch,
        compiler_params=params(),
        name="correct_inner",
    )(inner, swap, own_rows, *inner_weights)
    return pl.pallas_call(
        functools.partial(correct_outer, chunk),
        out_shape=shape((4, 2, length), F32),
        out_specs=pl.BlockSpec(memory_space=pltpu.HBM),
        scratch_shapes=scratch
        + [pltpu.VMEM((4, 2, length), F32), pltpu.SemaphoreType.DMA((length // chunk,))],
        compiler_params=params(),
        name="correct_outer",
    )(outer, swap, edge, cross, own_rows, row, *outer_weights)


def solution(mesh):
    placed = (
        P("section", "wide", None),
        P("wide", None),
        P("wide", None),
        P("wide", None),
        P("section", "wide", None),
        P("section", "wide", None),
        P(),
        P(),
        P(),
        P(),
        P(),
        P(),
    )
    return jax.shard_map(
        shards,
        mesh=mesh,
        in_specs=placed,
        out_specs=P(None, ("wide", "section"), None),
        check_vma=False,
    )
```
